512 devices in a mesh: frame: 16 (over y, z_hi), seq: 32 (over z_lo, x, core).
Axes of the slice: x: 4, y: 8, z: 8 (z_hi: 2, z_lo: 4; z = z_hi * 4 + z_lo), core: 2. Of those that a mesh axis runs over, the one named last changes fastest.
Arguments:
- vid_q: bfloat16 [16, 1024, 2048], P('frame', 'seq'), may hold values from -6 to 6
- vid_k: bfloat16 [16, 1024, 2048], P('frame', 'seq'), may hold values from -6 to 6
- vid_v: bfloat16 [16, 1024, 2048], P('frame', 'seq'), may hold values from -6 to 6
- vid_dout: bfloat16 [16, 1024, 2048], P('frame', 'seq'), may hold values from -6 to 6
- aud_q: bfloat16 [16, 3072, 2048], P('frame', 'seq'), may hold values from -6 to 6
- aud_k: bfloat16 [16, 3072, 2048], P('frame', 'seq'), may hold values from -6 to 6
- aud_v: bfloat16 [16, 3072, 2048], P('frame', 'seq'), may hold values from -6 to 6
- aud_dout: bfloat16 [16, 3072, 2048], P('frame', 'seq'), may hold values from -6 to 6
- aud_len: int32 [16, 32], replicated, may hold values from 32 to 96, as said below
- match: int32 [16], replicated, may hold values from 0 to 15, each once
Outputs:
- d_vid_q: bfloat16 [16, 1024, 2048], P('frame', 'seq')
- d_vid_k: bfloat16 [16, 1024, 2048], P('frame', 'seq')
- d_vid_v: bfloat16 [16, 1024, 2048], P('frame', 'seq')
- d_aud_q: bfloat16 [16, 3072, 2048], P('frame', 'seq')
- d_aud_k: bfloat16 [16, 3072, 2048], P('frame', 'seq')
- d_aud_v: bfloat16 [16, 3072, 2048], P('frame', 'seq')
The draws below stay inside these ranges and needn't reach their ends.
Inputs may be any that keep to these rules, and one draw needn't show every extreme that they name: `aud_len`: every entry is a whole multiple of 32; in every frame group one time block has 96 live slots and another has 32. match names every frame group once.
All inputs are finite; a program needn't handle non-finite values.
Results may differ from the reference program's by a relative error of at most 0.012.
The reference program's roundings to bfloat16 on the way count: a program that leaves them out, or rounds other values in their place, can miss the bound.
Values may be sent and summed in bfloat16 or wider, within the bound.
No kernel may reach another device: no remote copies, remote signals or barrier semaphores. Data moves between devices by JAX's collectives and lax.ppermute only.
A program may use at most 64 MiB of HBM per device.

```python
import jax
import jax.numpy as jnp
from jax import lax

HEADS = 16
HD = 128
VDEV = 32
ATILE = 32
LTILES = 3
BAND = 2
ACAP = 96
FRAMES = 16
SEQS = 32
VTOK = 1024
ATOK = 3072


def draw_aud_len(key, part):
    tiles = jax.random.randint(jax.random.fold_in(key, 11), (FRAMES, SEQS), 1, LTILES + 1)
    first = jax.random.randint(jax.random.fold_in(key, 12), (FRAMES,), 0, SEQS)
    stride = jax.random.randint(jax.random.fold_in(key, 13), (FRAMES,), 1, SEQS)
    second = (first + stride) % SEQS
    columns = jnp.arange(SEQS)[None, :]
    tiles = jnp.where(columns == first[:, None], LTILES, tiles)
    tiles = jnp.where(columns == second[:, None], 1, tiles)
    return (tiles * ATILE).astype(jnp.int32)


def drawn_rows(key, own, rows):
    values = jax.random.normal(jax.random.fold_in(key, own), (FRAMES, SEQS * rows, HEADS * HD), jnp.float32)
    return jnp.clip(values, -6.0, 6.0)


def draw_vid_q(key, part):
    values = drawn_rows(key, 21, VDEV)
    return values.astype(jnp.bfloat16)


def draw_aud_k(key, part):
    values = drawn_rows(key, 22, ACAP)
    return values.astype(jnp.bfloat16)


def draw_aud_q(key, part):
    values = drawn_rows(key, 23, ACAP)
    return values.astype(jnp.bfloat16)


def draw_vid_k(key, part):
    values = drawn_rows(key, 24, VDEV)
    return values.astype(jnp.bfloat16)


def level_of(stream_key, shape, split, low, high):
    def one(dim, shards_of):
        steps = jax.random.uniform(jax.random.fold_in(jax.random.fold_in(stream_key, 6), dim), (shards_of,), jnp.float32, low / len(split), high / len(split))
        return jnp.repeat(jnp.exp(steps), shape[dim] // shards_of).reshape((-1,) + (1,) * (len(shape) - dim - 1))

    level = one(*split[0])
    for cut in split[1:]:
        level = level * one(*cut)
    return level


def scatter_about(rng, extent, spread, bound, shards=(), kind=jnp.bfloat16):
    values = jax.random.normal(rng, extent, jnp.float32) * spread
    if len(shards) > 0:
        values = level_of(rng, extent, shards, -0.22, 0.18) * values
    return jnp.clip(values, min=-bound, max=bound).astype(kind)


def setup_inputs(seed: int = 0) -> dict:
    key_list = jax.random.split(jax.random.key(seed), 11)
    return {
        "vid_q": draw_vid_q(jax.random.fold_in(key_list[10], 71), 0),
        "vid_k": draw_vid_k(jax.random.fold_in(key_list[10], 71), 0),
        "vid_v": scatter_about(key_list[2], (FRAMES, VTOK, HEADS * HD), 1.0, 6.0, ((0, 16), (1, 32))),
        "vid_dout": scatter_about(key_list[3], (FRAMES, VTOK, HEADS * HD), 1.0, 6.0, ((0, 16), (1, 32))),
        "aud_q": draw_aud_q(jax.random.fold_in(key_list[10], 71), 0),
        "aud_k": draw_aud_k(jax.random.fold_in(key_list[10], 71), 0),
        "aud_v": scatter_about(key_list[6], (FRAMES, ATOK, HEADS * HD), 1.0, 6.0, ((0, 16), (1, 32))),
        "aud_dout": scatter_about(key_list[7], (FRAMES, ATOK, HEADS * HD), 1.0, 6.0, ((0, 16), (1, 32))),
        "aud_len": draw_aud_len(jax.random.fold_in(key_list[10], 71), 0),
        "match": jax.random.permutation(key_list[9], FRAMES).astype(jnp.int32),
    }


NEG_BIG = -1e30


def window(blocks):
    padded = jnp.pad(blocks, [(BAND, BAND)] + [(0, 0)] * (blocks.ndim - 1))
    count = blocks.shape[0]
    return jnp.concatenate([padded[position:position + count] for position in range(2 * BAND + 1)], axis=1)


def attend_pair(queries, key_rows, val_rows, grad_out, key_mask):
    factor = HD ** -0.5
    single = jnp.float32
    query_wide = queries.astype(single)
    key_wide = key_rows.astype(single)
    value_wide = val_rows.astype(single)
    grad_wide = grad_out.astype(single)
    scores = jnp.einsum('bqhd,bkhd->bhqk', query_wide, key_wide) * factor
    scores = jnp.where(key_mask[:, None, None, :], scores, NEG_BIG)
    largest = jnp.max(scores, axis=-1, keepdims=True)
    exponent = jnp.exp(scores - largest)
    weights = exponent / jnp.sum(exponent, axis=-1, keepdims=True)
    weights_half = weights.astype(jnp.bfloat16)
    weights_back = weights_half.astype(single)
    output = jnp.einsum('bhqk,bkhd->bqhd', weights_back, value_wide)
    deltas = jnp.transpose(jnp.sum(grad_wide * output, axis=-1), (0, 2, 1))[..., None]
    grad_weights = jnp.einsum('bqhd,bkhd->bhqk', grad_wide, value_wide)
    grad_scores = (weights * (grad_weights - deltas)).astype(jnp.bfloat16)
    scores_back = grad_scores.astype(single)
    grad_query = jnp.einsum('bhqk,bkhd->bqhd', scores_back, key_wide) * factor
    grad_key = jnp.einsum('bhqk,bqhd->bkhd', scores_back, query_wide) * factor
    grad_value = jnp.einsum('bhqk,bqhd->bkhd', weights_back, grad_wide)
    return grad_query, grad_key, grad_value


def owner_sum(part, rows):
    count = part.shape[0]
    span = 2 * BAND + 1
    pieces = part.reshape((count, span, rows) + part.shape[2:])
    rounded = lax.optimization_barrier(pieces.astype(jnp.bfloat16)).astype(jnp.float32)
    result = jnp.zeros((count, rows) + part.shape[2:], jnp.float32)
    for position in range(span):
        padded = jnp.pad(rounded[:, position], [(BAND, BAND)] + [(0, 0)] * (part.ndim - 1))
        result = result + padded[2 * BAND - position:2 * BAND - position + count]
    return result


def reference(vid_q, vid_k, vid_v, vid_dout, aud_q, aud_k, aud_v, aud_dout, aud_len, match):
    order = jnp.arange(FRAMES, dtype=jnp.int32)
    inverse = jnp.sum(jnp.where(match[None, :] == order[:, None], order[None, :], 0), axis=1).astype(jnp.int32)
    lengths = jnp.take(aud_len, match, axis=0)
    slots = jnp.arange(ACAP, dtype=jnp.int32)
    audio_mask = slots[None, None, :] < lengths[:, :, None]

    def blocks(array, rows):
        return array.reshape(FRAMES, SEQS, rows, HEADS, HD)

    def paired(array):
        return blocks(jnp.take(array, match, axis=0), ACAP)

    audio_grad = jnp.where(audio_mask[..., None, None], paired(aud_dout), jnp.zeros((), jnp.bfloat16))
    video_mask = window(jnp.ones((SEQS, VDEV), jnp.float32)) > 0.5

    def one_frame(items):
        video_query, video_key, video_value, video_grad, audio_query, audio_key, audio_value, audio_cot, audio_live = items
        audio_window = window(audio_live.astype(jnp.float32)) > 0.5
        grad_vq, grad_ak, grad_av = attend_pair(video_query, window(audio_key), window(audio_value), video_grad, audio_window)
        grad_aq, grad_vk, grad_vv = attend_pair(audio_query, window(video_key), window(video_value), audio_cot, video_mask)
        return (grad_vq, owner_sum(grad_vk, VDEV), owner_sum(grad_vv, VDEV),
                grad_aq, owner_sum(grad_ak, ACAP), owner_sum(grad_av, ACAP))

    results = lax.map(one_frame, (blocks(vid_q, VDEV), blocks(vid_k, VDEV), blocks(vid_v, VDEV), blocks(vid_dout, VDEV),
                                  paired(aud_q), paired(aud_k), paired(aud_v), audio_grad, audio_mask))

    def finish(array, rows):
        return array.reshape(FRAMES, SEQS * rows, HEADS * HD).astype(jnp.bfloat16)

    def unpair(array):
        return jnp.take(finish(array, ACAP), inverse, axis=0)

    return (finish(results[0], VDEV), finish(results[1], VDEV), finish(results[2], VDEV),
            unpair(results[3]), unpair(results[4]), unpair(results[5]))
```

```python
import functools

import jax
import jax.numpy as jnp
from jax import lax
from jax.experimental import pallas as pl
from jax.experimental.pallas import tpu as pltpu
from jax.sharding import PartitionSpec as P

HD = 128
BAND = 2
NEG_BIG = -1e30
FACTOR = HD ** (-0.5)
HEADS_PER_STEP = 2
INTERPRET = False


def attend(queries, keys, values, grads, mask):
    scores = (
        lax.dot_general(
            queries, keys, (((1,), (1,)), ((), ())), preferred_element_type=jnp.float32
        )
        * FACTOR
    )
    scores = jnp.where(mask, scores, NEG_BIG)
    largest = jnp.max(scores, axis=-1, keepdims=True)
    exponent = jnp.exp(scores - largest)
    weights = exponent * (1.0 / jnp.sum(exponent, axis=-1, keepdims=True))
    half = weights.astype(jnp.bfloat16)
    grad_weights = lax.dot_general(
        grads, values, (((1,), (1,)), ((), ())), preferred_element_type=jnp.float32
    )
    delta = jnp.sum(half.astype(jnp.float32) * grad_weights, axis=-1, keepdims=True)
    grad_scores = (weights * (grad_weights - delta)).astype(jnp.bfloat16)
    grad_query = (
        lax.dot_general(
            grad_scores, keys, (((1,), (0,)), ((), ())), preferred_element_type=jnp.float32
        )
        * FACTOR
    )
    key_terms = (
        lax.dot_general(
            grad_scores, queries, (((0,), (0,)), ((), ())), preferred_element_type=jnp.float32
        )
        * FACTOR
    )
    value_terms = lax.dot_general(
        half, grads, (((0,), (0,)), ((), ())), preferred_element_type=jnp.float32
    )
    return grad_query, key_terms, value_terms


def video_kernel(group, mask_ref, q_ref, g_ref, before, here, after, dq_ref, tb, th, ta):
    rows = q_ref.shape[0]
    part = before.shape[0] // 2
    late = (lax.broadcasted_iota(jnp.int32, (rows, 1), 0) // group) % 2
    mask = jnp.where(late == 0, mask_ref[0:1, :], mask_ref[1:2, :]) > 0
    for head in range(q_ref.shape[1] // HD):
        cols = slice(head * HD, (head + 1) * HD)
        keys = jnp.concatenate([ref[:part, cols] for ref in (before, here, after)], axis=0)
        values = jnp.concatenate([ref[part:, cols] for ref in (before, here, after)], axis=0)
        dq, kt, vt = attend(q_ref[:, cols], keys, values, g_ref[:, cols], mask)
        dq_ref[:, cols] = dq.astype(jnp.bfloat16)
        for place, out in enumerate((tb, th, ta)):
            span = slice(place * part, (place + 1) * part)
            out[:part, cols] = kt[span].astype(jnp.bfloat16)
            out[part:, cols] = vt[span].astype(jnp.bfloat16)


def audio_kernel(
    info, mask_ref, q_mine, g_mine, q_other, g_other, before, here, after, dq_ref, tb, th, ta
):
    rows = q_mine.shape[0]
    part = before.shape[0] // 2
    keys_total = 3 * part
    slot = lax.broadcasted_iota(jnp.int32, (rows, 1), 0)
    live_mine = slot < info[1]
    live_other = slot < info[2]
    mask = jnp.concatenate(
        [
            jnp.broadcast_to(mask_ref[0:1, :], (rows, keys_total)),
            jnp.broadcast_to(mask_ref[1:2, :], (rows, keys_total)),
        ],
        axis=0,
    )
    mask = mask > 0
    for head in range(q_mine.shape[1] // HD):
        cols = slice(head * HD, (head + 1) * HD)
        queries = jnp.concatenate([q_mine[:, cols], q_other[:, cols]], axis=0)
        zero = jnp.zeros((), jnp.bfloat16)
        grads = jnp.concatenate(
            [
                jnp.where(live_mine, g_mine[:, cols], zero),
                jnp.where(live_other, g_other[:, cols], zero),
            ],
            axis=0,
        )
        keys = jnp.concatenate([ref[:part, cols] for ref in (before, here, after)], axis=0)
        values = jnp.concatenate([ref[part:, cols] for ref in (before, here, after)], axis=0)
        dq, kt, vt = attend(queries, keys, values, grads, mask)
        dq_ref[:, cols] = dq.astype(jnp.bfloat16)
        for place, out in enumerate((tb, th, ta)):
            span = slice(place * part, (place + 1) * part)
            out[:part, cols] = kt[span].astype(jnp.bfloat16)
            out[part:, cols] = vt[span].astype(jnp.bfloat16)


def cost(rows, keys, width):
    heads = width // HD
    return pl.CostEstimate(
        flops=10 * rows * keys * HD * heads,
        bytes_accessed=2 * width * (4 * rows + 4 * keys),
        transcendentals=rows * keys * heads,
    )


def video_side(mask, video, before, here, after, group):
    width = video.shape[1]
    rows = video.shape[0] // 4
    wide = min(HEADS_PER_STEP * HD, width)
    window = before.shape[0]
    column = lambda h: (0, h)
    kv = pl.BlockSpec((window, wide), column)
    bf = jnp.bfloat16
    return pl.pallas_call(
        functools.partial(video_kernel, group),
        grid=(width // wide,),
        in_specs=[
            pl.BlockSpec(mask.shape, lambda h: (0, 0)),
            pl.BlockSpec((rows, wide), column),
            pl.BlockSpec((rows, wide), lambda h: (3, h)),
            kv,
            kv,
            kv,
        ],
        out_specs=[pl.BlockSpec((rows, wide), column), kv, kv, kv],
        out_shape=[jax.ShapeDtypeStruct((rows, width), bf)]
        + [jax.ShapeDtypeStruct((window, width), bf)] * 3,
        cost_estimate=cost(rows, 3 * window // 2, width),
        name="video_side",
        interpret=INTERPRET,
    )(mask, video, video, before, here, after)


def audio_side(info, mask, aud_q, aud_g, theirs, before, here, after):
    width = theirs.shape[1]
    rows = aud_q.shape[0]
    wide = min(HEADS_PER_STEP * HD, width)
    steps = width // wide
    window = before.shape[0]
    kv = pl.BlockSpec((window, wide), lambda h, info: (0, h))
    mine = pl.BlockSpec((rows, wide), lambda h, info: (0, info[0] * steps + h))
    bf = jnp.bfloat16
    return pl.pallas_call(
        audio_kernel,
        grid_spec=pltpu.PrefetchScalarGridSpec(
            num_scalar_prefetch=1,
            grid=(steps,),
            in_specs=[
                pl.BlockSpec(mask.shape, lambda h, info: (0, 0)),
                mine,
                mine,
                pl.BlockSpec((rows, wide), lambda h, info: (0, h)),
                pl.BlockSpec((rows, wide), lambda h, info: (3, h)),
                kv,
                kv,
                kv,
            ],
            out_specs=[pl.BlockSpec((2 * rows, wide), lambda h, info: (0, h)), kv, kv, kv],
        ),
        out_shape=[jax.ShapeDtypeStruct((2 * rows, width), bf)]
        + [jax.ShapeDtypeStruct((window, width), bf)] * 3,
        cost_estimate=cost(2 * rows, 3 * window // 2, width),
        name="audio_side",
        interpret=INTERPRET,
    )(info, mask, aud_q, aud_g, theirs, theirs, before, here, after)


def shards(vid_q, vid_k, vid_v, vid_dout, aud_q, aud_k, aud_v, aud_dout, aud_len, match):
    frames = lax.axis_size("frame")
    count = lax.axis_size("seq")
    group_here = lax.axis_index("frame")
    block_here = lax.axis_index("seq")
    core = block_here % 2
    base = block_here - core
    video_rows, width = vid_q.shape[1], vid_q.shape[2]
    audio_rows = aud_q.shape[1]
    half = width // 2
    group = 4 * video_rows // frames
    runs = frames // 4
    spreads = frames // runs
    slim = half // spreads
    f32, bf = jnp.float32, jnp.bfloat16

    pairs = [
        [f * count + 2 * c + k for f in range(frames) for k in range(2)]
        for c in range(count // 2)
    ]

    def pair_exchange(x):
        return lax.all_to_all(
            x, ("frame", "seq"), split_axis=0, concat_axis=0, tiled=True, axis_index_groups=pairs
        )

    def exchange(x):
        return lax.all_to_all(x, "frame", split_axis=0, concat_axis=0, tiled=True)

    def shift(x, by):
        return lax.ppermute(
            x, "seq", [(i, i + by) for i in range(count) if 0 <= i + by < count]
        )

    def swap(x):
        return lax.ppermute(x, "seq", [(i, i ^ 1) for i in range(count)])

    order = jnp.arange(frames, dtype=jnp.int32)
    inverse = jnp.sum(
        jnp.where(match[None, :] == order[:, None], order[None, :], 0), axis=1
    ).astype(jnp.int32)

    packed = jnp.concatenate([vid_q[0], vid_k[0], vid_v[0], vid_dout[0]], axis=0)
    packed = packed.reshape(frames, group, 2, half).transpose(0, 2, 1, 3)
    spread = pair_exchange(packed.reshape(2 * frames, group, half))
    spread = jnp.take(spread.reshape(frames, 2 * group, half), inverse, axis=0, mode="clip")
    video = exchange(spread).reshape(frames * 2 * group, half)

    def halves(x):
        low, high = x[0, :, :half], x[0, :, half:]
        return jnp.where(core == 0, low, high), jnp.where(core == 0, high, low)

    own_k, send_k = halves(aud_k)
    own_v, send_v = halves(aud_v)
    send_q = halves(aud_q)[1]
    send_g = halves(aud_dout)[1]
    theirs = swap(jnp.concatenate([send_q, send_k, send_v, send_g], axis=0))
    audio_here = jnp.concatenate(
        [
            own_k,
            theirs[audio_rows : 2 * audio_rows],
            own_v,
            theirs[2 * audio_rows : 3 * audio_rows],
        ],
        axis=0,
    )
    audio_before = shift(audio_here, 2)
    audio_after = shift(audio_here, -2)

    lengths = lax.dynamic_index_in_dim(aud_len, group_here, 0, keepdims=False)
    audio_offsets = jnp.stack(
        [-2 + core, -1 - core, core, 1 - core, 2 + core, 3 - core]
    )
    audio_times = base + audio_offsets
    audio_live = jnp.where(
        (audio_times >= 0) & (audio_times < count),
        jnp.take(lengths, audio_times, mode="clip"),
        0,
    )
    slots = jnp.arange(audio_rows, dtype=jnp.int32)
    live = slots[None, :] < audio_live[:, None]
    late = jnp.arange(2, dtype=jnp.int32)
    near = jnp.abs(late[:, None] - audio_offsets[None, :]) <= BAND
    video_mask = (near[:, :, None] & live[None]).reshape(2, 6 * audio_rows).astype(jnp.int32)

    column = jnp.arange(6 * video_rows, dtype=jnp.int32)
    video_offsets = 2 * (column // (2 * video_rows)) - 2 + (column // group) % 2
    video_times = base + video_offsets
    own_offsets = jnp.stack([core, 1 - core])
    audio_mask = (
        (jnp.abs(own_offsets[:, None] - video_offsets[None, :]) <= BAND)
        & (video_times >= 0)[None]
        & (video_times < count)[None]
    ).astype(jnp.int32)
    info = jnp.stack([core, audio_live[2], audio_live[3]]).astype(jnp.int32)

    block = 2 * video_rows
    video_here = video[block : 3 * block]
    video_before = shift(video_here, 2)
    video_after = shift(video_here, -2)
    grad_vq, audio_tb, audio_th, audio_ta = video_side(
        video_mask, video, audio_before, audio_here, audio_after, group
    )
    grad_aq, video_tb, video_th, video_ta = audio_side(
        info, audio_mask, aud_q[0], aud_dout[0], theirs, video_before, video_here, video_after
    )

    grad_vkv = (
        video_th.astype(f32)
        + shift(video_tb, -2).astype(f32)
        + shift(video_ta, 2).astype(f32)
    ).astype(bf)
    grads = jnp.concatenate([grad_vq, grad_vkv], axis=0)
    grads = grads.reshape(3, runs, 2, group, spreads, slim).transpose(1, 4, 2, 0, 3, 5)
    grads = exchange(grads.reshape(frames, 6 * group, slim))
    grads = jnp.take(grads, match, axis=0, mode="clip")
    grads = pair_exchange(grads.reshape(2 * frames, 3 * group, slim))
    grads = grads.reshape(runs, spreads, 2, 3, group, slim).transpose(3, 0, 4, 2, 1, 5)
    grads = grads.reshape(3, video_rows, width)

    grad_akv = (
        audio_th.astype(f32)
        + shift(audio_tb, -2).astype(f32)
        + shift(audio_ta, 2).astype(f32)
    ).astype(bf)
    mine = (
        grad_aq[:audio_rows],
        grad_akv[:audio_rows],
        grad_akv[2 * audio_rows : 3 * audio_rows],
    )
    back = swap(
        jnp.concatenate(
            [
                grad_aq[audio_rows:],
                grad_akv[audio_rows : 2 * audio_rows],
                grad_akv[3 * audio_rows :],
            ],
            axis=0,
        )
    )

    def whole(own, other):
        return jnp.where(
            core == 0,
            jnp.concatenate([own, other], axis=1),
            jnp.concatenate([other, own], axis=1),
        )[None]

    outs = [
        whole(mine[j], back[j * audio_rows : (j + 1) * audio_rows]) for j in range(3)
    ]
    return (grads[0][None], grads[1][None], grads[2][None], outs[0], outs[1], outs[2])


def solution(mesh):
    tokens = P("frame", "seq", None)
    return jax.shard_map(
        shards,
        mesh=mesh,
        in_specs=(tokens,) * 8 + (P(), P()),
        out_specs=(tokens,) * 6,
        check_vma=False,
    )
```

```python
import functools

import jax
import jax.numpy as jnp
from jax import lax
from jax.experimental import pallas as pl
from jax.experimental.pallas import tpu as pltpu
from jax.sharding import PartitionSpec as P


HD = 128
BAND = 2
NEG_BIG = -1e30
FACTOR = HD ** (-0.5)
HEADS_PER_STEP = 2
INTERPRET = False


def attend(queries, keys, values, grads, bias):
    scores = (
        lax.dot_general(
            queries, keys, (((1,), (1,)), ((), ())), preferred_element_type=jnp.float32
        )
        * FACTOR
    )
    scores = scores + bias
    largest = jnp.max(scores, axis=-1, keepdims=True)
    exponent = jnp.exp(scores - largest)
    weights = exponent * (1.0 / jnp.sum(exponent, axis=-1, keepdims=True))
    half = weights.astype(jnp.bfloat16)
    grad_weights = lax.dot_general(
        grads, values, (((1,), (1,)), ((), ())), preferred_element_type=jnp.float32
    )
    delta = jnp.sum(half.astype(jnp.float32) * grad_weights, axis=-1, keepdims=True)
    grad_scores = (weights * (grad_weights - delta)).astype(jnp.bfloat16)
    grad_query = (
        lax.dot_general(
            grad_scores, keys, (((1,), (0,)), ((), ())), preferred_element_type=jnp.float32
        )
        * FACTOR
    )
    key_terms = (
        lax.dot_general(
            grad_scores, queries, (((0,), (0,)), ((), ())), preferred_element_type=jnp.float32
        )
        * FACTOR
    )
    value_terms = lax.dot_general(
        half, grads, (((0,), (0,)), ((), ())), preferred_element_type=jnp.float32
    )
    return grad_query, key_terms, value_terms


def video_kernel(group, count, lens, queries, grads, before, here, after, dq_ref, tb, th, ta, bias):
    part = before.shape[0] // 2

    @pl.when(pl.program_id(0) == 0)
    def _():
        video_bias(group, count, lens, part, bias)

    def one(head):
        cols = slice(head * HD, (head + 1) * HD)
        keys = jnp.concatenate([ref[:part, cols] for ref in (before, here, after)], axis=0)
        values = jnp.concatenate([ref[part:, cols] for ref in (before, here, after)], axis=0)
        dq, kt, vt = attend(queries[:, cols], keys, values, grads[:, cols], bias[...])
        dq_ref[:, cols] = dq.astype(jnp.bfloat16)
        for place, out in enumerate((tb, th, ta)):
            span = slice(place * part, (place + 1) * part)
            out[:part, cols] = kt[span].astype(jnp.bfloat16)
            out[part:, cols] = vt[span].astype(jnp.bfloat16)

    for head in range(dq_ref.shape[1] // HD):
        one(head)


def video_bias(group, count, lens, part, bias):
    rows, slots = bias.shape[0], part // 2
    frame = lax.axis_index("frame")
    block = lax.axis_index("seq")
    core = lax.rem(block, 2)
    base = block - core
    column = lax.broadcasted_iota(jnp.int32, (1, 3 * part), 1)
    early_row = jnp.full((1, 3 * part), NEG_BIG, jnp.float32)
    late_row = early_row
    for place in range(6):
        offset = 2 * (place // 2) - 2 + (core if place % 2 == 0 else 1 - core)
        time = base + offset
        known = (time >= 0) & (time < count)
        live = lens[frame, jnp.clip(time, 0, count - 1)]
        live = jnp.where(known, live, 0)
        early = jnp.where(jnp.abs(offset) <= BAND, live, 0)
        late = jnp.where(jnp.abs(offset - 1) <= BAND, live, 0)
        first = column >= place * slots
        early_row = jnp.where(first & (column < place * slots + early), 0.0, early_row)
        late_row = jnp.where(first & (column < place * slots + late), 0.0, late_row)
    is_late = (lax.broadcasted_iota(jnp.int32, (rows, 1), 0) // group) % 2
    bias[...] = jnp.where(is_late == 0, early_row, late_row)


def audio_kernel(
    group, count, lens, aud_q, aud_g, their_q, their_g, before, here, after, dq_ref, tb, th, ta, bias
):
    rows, half = aud_q.shape[0], aud_q.shape[1] // 2
    wide = their_q.shape[1]
    part = before.shape[0] // 2
    frame = lax.axis_index("frame")
    block = lax.axis_index("seq")
    core = lax.rem(block, 2)
    base = block - core
    other = base + 1 - core
    column = lax.broadcasted_iota(jnp.int32, (1, 3 * part), 1)
    offset = 2 * (column // part) - 2 + (column // group) % 2
    known = (base + offset >= 0) & (base + offset < count)

    @pl.when(pl.program_id(0) == 0)
    def _():
        for j, own in enumerate((core, 1 - core)):
            seen = known & (jnp.abs(offset - own) <= BAND)
            bias[j * rows : (j + 1) * rows] = jnp.broadcast_to(
                jnp.where(seen, 0.0, NEG_BIG), (rows, 3 * part)
            )

    slot = lax.broadcasted_iota(jnp.int32, (rows, 1), 0)
    live_mine = (slot < lens[frame, block]).astype(jnp.float32)
    live_other = (slot < lens[frame, other]).astype(jnp.float32)

    def one(head):
        cols = slice(head * HD, (head + 1) * HD)
        start = core * half + pl.program_id(0) * wide + head * HD
        mine = pl.ds(pl.multiple_of(start, HD), HD)
        queries = jnp.concatenate([aud_q[:, mine], their_q[:, cols]], axis=0)
        zero = jnp.zeros((), jnp.float32)
        grads = jnp.concatenate(
            [
                jnp.where(live_mine > 0, aud_g[:, mine].astype(jnp.float32), zero),
                jnp.where(live_other > 0, their_g[:, cols].astype(jnp.float32), zero),
            ],
            axis=0,
        ).astype(jnp.bfloat16)
        keys = jnp.concatenate([ref[:part, cols] for ref in (before, here, after)], axis=0)
        values = jnp.concatenate([ref[part:, cols] for ref in (before, here, after)], axis=0)
        dq, kt, vt = attend(queries, keys, values, grads, bias[...])
        dq_ref[:, cols] = dq.astype(jnp.bfloat16)
        for place, out in enumerate((tb, th, ta)):
            span = slice(place * part, (place + 1) * part)
            out[:part, cols] = kt[span].astype(jnp.bfloat16)
            out[part:, cols] = vt[span].astype(jnp.bfloat16)

    for head in range(wide // HD):
        one(head)


def cost(rows, keys, width):
    heads_here = width // HD
    return pl.CostEstimate(
        flops=10 * rows * keys * HD * heads_here,
        bytes_accessed=2 * width * (4 * rows + 4 * keys),
        transcendentals=rows * keys * heads_here,
    )


ON_CHIP = pl.BlockSpec(memory_space=pltpu.VMEM)
GRANT = 20 * 2**20
SCALARS = pl.BlockSpec(memory_space=pltpu.SMEM)


def side(kernel, lens, operands, specs, rows, window, width):
    bf = jnp.bfloat16
    wide = min(HEADS_PER_STEP * HD, width)
    return pl.pallas_call(
        kernel,
        grid=(width // wide,),
        in_specs=[SCALARS] + specs,
        out_specs=[columns(rows, wide)] + [columns(window, wide)] * 3,
        out_shape=[jax.ShapeDtypeStruct((rows, width), bf)]
        + [jax.ShapeDtypeStruct((window, width), bf)] * 3,
        scratch_shapes=[pltpu.VMEM((rows, 3 * window // 2), jnp.float32)],
        compiler_params=pltpu.CompilerParams(vmem_limit_bytes=GRANT),
        cost_estimate=cost(rows, 3 * window // 2, width),
        interpret=INTERPRET,
    )(lens, *operands)


def columns(rows, wide, row=0):
    return pl.BlockSpec((rows, wide), lambda h: (row, h))


def assemble_kernel(runs, spreads, group, x, *outs):
    slim = x.shape[2]
    for run in range(runs):
        for spread in range(spreads):
            for core in range(2):
                piece = (run * spreads + spread) * 2 + core
                for j, out in enumerate(outs):
                    left = (core * spreads + spread) * slim
                    out[0, run * group : (run + 1) * group, left : left + slim] = x[
                        piece, j * group : (j + 1) * group, :
                    ]


def assemble(x, runs, spreads, group):
    shape = (1, runs * group, 2 * spreads * x.shape[2])
    return pl.pallas_call(
        functools.partial(assemble_kernel, runs, spreads, group),
        in_specs=[ON_CHIP],
        out_specs=[ON_CHIP] * 3,
        out_shape=[jax.ShapeDtypeStruct(shape, jnp.bfloat16)] * 3,
        compiler_params=pltpu.CompilerParams(vmem_limit_bytes=GRANT),
        name="assemble",
        interpret=INTERPRET,
    )(x)


def shards(vid_q, vid_k, vid_v, vid_dout, aud_q, aud_k, aud_v, aud_dout, aud_len, match):
    frames = lax.axis_size("frame")
    count = lax.axis_size("seq")
    block_here = lax.axis_index("seq")
    core = block_here % 2
    video_rows, width = vid_q.shape[1], vid_q.shape[2]
    audio_rows = aud_q.shape[1]
    half = width // 2
    group = 4 * video_rows // frames
    runs = frames // 4
    spreads = frames // runs
    slim = half // spreads
    f32, bf = jnp.float32, jnp.bfloat16

    pairs = [
        [f * count + 2 * c + k for f in range(frames) for k in range(2)]
        for c in range(count // 2)
    ]

    def pair_exchange(x):
        return lax.all_to_all(
            x, ("frame", "seq"), split_axis=0, concat_axis=0, tiled=True, axis_index_groups=pairs
        )

    def exchange(x):
        return lax.all_to_all(x, "frame", split_axis=0, concat_axis=0, tiled=True)

    def shift(x, by):
        return lax.ppermute(
            x, "seq", [(i, i + by) for i in range(count) if 0 <= i + by < count]
        )

    def swap(x):
        return lax.ppermute(x, "seq", [(i, i ^ 1) for i in range(count)])

    order = jnp.arange(frames, dtype=jnp.int32)
    inverse = jnp.sum(
        jnp.where(match[None, :] == order[:, None], order[None, :], 0), axis=1
    ).astype(jnp.int32)

    packed = jnp.concatenate([vid_q[0], vid_k[0], vid_v[0], vid_dout[0]], axis=0)
    packed = packed.reshape(frames, group, 2, half).transpose(0, 2, 1, 3)
    spread = pair_exchange(packed.reshape(2 * frames, group, half))
    spread = jnp.take(spread.reshape(frames, 2 * group, half), inverse, axis=0, mode="clip")
    video = exchange(spread).reshape(frames * 2 * group, half)

    def halves(x):
        low, high = x[0, :, :half], x[0, :, half:]
        return jnp.where(core == 0, low, high), jnp.where(core == 0, high, low)

    own_k, send_k = halves(aud_k)
    own_v, send_v = halves(aud_v)
    send_q = halves(aud_q)[1]
    send_g = halves(aud_dout)[1]
    sent = jnp.concatenate([send_q, send_k, send_v, send_g], axis=0)
    theirs = swap(sent)
    audio_here = jnp.concatenate(
        [
            own_k,
            theirs[audio_rows : 2 * audio_rows],
            own_v,
            theirs[2 * audio_rows : 3 * audio_rows],
        ],
        axis=0,
    )
    audio_before = shift(audio_here, 2)
    audio_after = shift(audio_here, -2)

    block = 2 * video_rows
    video_here = video[block : 3 * block]
    video_before = shift(video_here, 2)
    video_after = shift(video_here, -2)
    wide = min(HEADS_PER_STEP * HD, half)
    full = pl.BlockSpec((audio_rows, width), lambda h: (0, 0))
    grad_vq, audio_tb, audio_th, audio_ta = side(
        functools.partial(video_kernel, group, count),
        aud_len,
        (video, video, audio_before, audio_here, audio_after),
        [columns(block, wide), columns(block, wide, 3)] + [columns(4 * audio_rows, wide)] * 3,
        block,
        4 * audio_rows,
        half,
    )
    grad_aq, video_tb, video_th, video_ta = side(
        functools.partial(audio_kernel, group, count),
        aud_len,
        (aud_q[0], aud_dout[0], theirs, theirs, video_before, video_here, video_after),
        [full, full, columns(audio_rows, wide), columns(audio_rows, wide, 3)]
        + [columns(2 * block, wide)] * 3,
        2 * audio_rows,
        2 * block,
        half,
    )

    grad_vkv = (
        video_th.astype(f32)
        + shift(video_tb, -2).astype(f32)
        + shift(video_ta, 2).astype(f32)
    ).astype(bf)
    grads = jnp.concatenate([grad_vq, grad_vkv], axis=0)
    grads = grads.reshape(3, runs, 2, group, spreads, slim).transpose(1, 4, 2, 0, 3, 5)
    grads = exchange(grads.reshape(frames, 6 * group, slim))
    grads = jnp.take(grads, match, axis=0, mode="clip")
    grads = pair_exchange(grads.reshape(2 * frames, 3 * group, slim))
    grads = assemble(grads, runs, spreads, group)

    from_after, from_before = shift(audio_tb, -2), shift(audio_ta, 2)
    grad_akv = (
        audio_th.astype(f32) + from_after.astype(f32) + from_before.astype(f32)
    ).astype(bf)
    mine = (
        grad_aq[:audio_rows],
        grad_akv[:audio_rows],
        grad_akv[2 * audio_rows : 3 * audio_rows],
    )
    back = swap(
        jnp.concatenate(
            [
                grad_aq[audio_rows:],
                grad_akv[audio_rows : 2 * audio_rows],
                grad_akv[3 * audio_rows :],
            ],
            axis=0,
        )
    )

    def whole(own, other):
        return jnp.where(
            core == 0,
            jnp.concatenate([own, other], axis=1),
            jnp.concatenate([other, own], axis=1),
        )[None]

    outs = [
        whole(mine[j], back[j * audio_rows : (j + 1) * audio_rows]) for j in range(3)
    ]
    return (*grads, *outs)


def solution(mesh):
    tokens = P("frame", "seq", None)
    return jax.shard_map(
        shards,
        mesh=mesh,
        in_specs=(tokens,) * 8 + (P(), P()),
        out_specs=(tokens,) * 6,
        check_vma=False,
    )
```

```python
import functools

import jax
import jax.numpy as jnp
from jax import lax
from jax.experimental import pallas as pl
from jax.experimental.pallas import tpu as pltpu
from jax.sharding import PartitionSpec as P


HD = 128
BAND = 2
NEG_BIG = -1e30
FACTOR = HD ** (-0.5)
HEADS_PER_STEP = 2
INTERPRET = False


def attend(queries, keys, values, grads, bias):
    scores = (
        lax.dot_general(
            queries, keys, (((1,), (1,)), ((), ())), preferred_element_type=jnp.float32
        )
        * FACTOR
    )
    scores = scores + bias
    largest = jnp.max(scores, axis=-1, keepdims=True)
    exponent = jnp.exp(scores - largest)
    weights = exponent * (1.0 / jnp.sum(exponent, axis=-1, keepdims=True))
    half = weights.astype(jnp.bfloat16)
    grad_weights = lax.dot_general(
        grads, values, (((1,), (1,)), ((), ())), preferred_element_type=jnp.float32
    )
    delta = jnp.sum(half.astype(jnp.float32) * grad_weights, axis=-1, keepdims=True)
    grad_scores = (weights * (grad_weights - delta)).astype(jnp.bfloat16)
    grad_query = (
        lax.dot_general(
            grad_scores, keys, (((1,), (0,)), ((), ())), preferred_element_type=jnp.float32
        )
        * FACTOR
    )
    key_terms = (
        lax.dot_general(
            grad_scores, queries, (((0,), (0,)), ((), ())), preferred_element_type=jnp.float32
        )
        * FACTOR
    )
    value_terms = lax.dot_general(
        half, grads, (((0,), (0,)), ((), ())), preferred_element_type=jnp.float32
    )
    return grad_query, key_terms, value_terms


def video_kernel(group, count, lens, queries, grads, before, here, after, dq_ref, tb, th, ta, bias):
    part = before.shape[0] // 2

    @pl.when(pl.program_id(0) == 0)
    def _():
        video_bias(group, count, lens, part, bias)

    def one(head):
        cols = slice(head * HD, (head + 1) * HD)
        keys = jnp.concatenate([ref[:part, cols] for ref in (before, here, after)], axis=0)
        values = jnp.concatenate([ref[part:, cols] for ref in (before, here, after)], axis=0)
        dq, kt, vt = attend(queries[:, cols], keys, values, grads[:, cols], bias[...])
        dq_ref[:, cols] = dq.astype(jnp.bfloat16)
        for place, out in enumerate((tb, th, ta)):
            span = slice(place * part, (place + 1) * part)
            out[:part, cols] = kt[span].astype(jnp.bfloat16)
            out[part:, cols] = vt[span].astype(jnp.bfloat16)

    for head in range(dq_ref.shape[1] // HD):
        one(head)


def video_bias(group, count, lens, part, bias):
    rows, slots = bias.shape[0], part // 2
    frame = lax.axis_index("frame")
    block = lax.axis_index("seq")
    core = lax.rem(block, 2)
    base = block - core
    column = lax.broadcasted_iota(jnp.int32, (1, 3 * part), 1)
    early_row = jnp.full((1, 3 * part), NEG_BIG, jnp.float32)
    late_row = early_row
    for place in range(6):
        offset = 2 * (place // 2) - 2 + (core if place % 2 == 0 else 1 - core)
        time = base + offset
        known = (time >= 0) & (time < count)
        live = lens[frame, jnp.clip(time, 0, count - 1)]
        live = jnp.where(known, live, 0)
        early = jnp.where(jnp.abs(offset) <= BAND, live, 0)
        late = jnp.where(jnp.abs(offset - 1) <= BAND, live, 0)
        first = column >= place * slots
        early_row = jnp.where(first & (column < place * slots + early), 0.0, early_row)
        late_row = jnp.where(first & (column < place * slots + late), 0.0, late_row)
    is_late = (lax.broadcasted_iota(jnp.int32, (rows, 1), 0) // group) % 2
    bias[...] = jnp.where(is_late == 0, early_row, late_row)


def audio_kernel(
    group, count, lens, aud_q, aud_g, their_q, their_g, before, here, after, dq_ref, tb, th, ta, bias
):
    rows, half = aud_q.shape[0], aud_q.shape[1] // 2
    wide = their_q.shape[1]
    part = before.shape[0] // 2
    frame = lax.axis_index("frame")
    block = lax.axis_index("seq")
    core = lax.rem(block, 2)
    base = block - core
    other = base + 1 - core
    column = lax.broadcasted_iota(jnp.int32, (1, 3 * part), 1)
    offset = 2 * (column // part) - 2 + (column // group) % 2
    known = (base + offset >= 0) & (base + offset < count)

    @pl.when(pl.program_id(0) == 0)
    def _():
        for j, own in enumerate((core, 1 - core)):
            seen = known & (jnp.abs(offset - own) <= BAND)
            bias[j * rows : (j + 1) * rows] = jnp.broadcast_to(
                jnp.where(seen, 0.0, NEG_BIG), (rows, 3 * part)
            )

    slot = lax.broadcasted_iota(jnp.int32, (rows, 1), 0)
    live_mine = (slot < lens[frame, block]).astype(jnp.float32)
    live_other = (slot < lens[frame, other]).astype(jnp.float32)

    def one(head):
        cols = slice(head * HD, (head + 1) * HD)
        start = core * half + pl.program_id(0) * wide + head * HD
        mine = pl.ds(pl.multiple_of(start, HD), HD)
        queries = jnp.concatenate([aud_q[:, mine], their_q[:, cols]], axis=0)
        zero = jnp.zeros((), jnp.float32)
        grads = jnp.concatenate(
            [
                jnp.where(live_mine > 0, aud_g[:, mine].astype(jnp.float32), zero),
                jnp.where(live_other > 0, their_g[:, cols].astype(jnp.float32), zero),
            ],
            axis=0,
        ).astype(jnp.bfloat16)
        keys = jnp.concatenate([ref[:part, cols] for ref in (before, here, after)], axis=0)
        values = jnp.concatenate([ref[part:, cols] for ref in (before, here, after)], axis=0)
        dq, kt, vt = attend(queries, keys, values, grads, bias[...])
        dq_ref[:, cols] = dq.astype(jnp.bfloat16)
        for place, out in enumerate((tb, th, ta)):
            span = slice(place * part, (place + 1) * part)
            out[:part, cols] = kt[span].astype(jnp.bfloat16)
            out[part:, cols] = vt[span].astype(jnp.bfloat16)

    for head in range(wide // HD):
        one(head)


def cost(rows, keys, width):
    heads_here = width // HD
    return pl.CostEstimate(
        flops=10 * rows * keys * HD * heads_here,
        bytes_accessed=2 * width * (4 * rows + 4 * keys),
        transcendentals=rows * keys * heads_here,
    )


ON_CHIP = pl.BlockSpec(memory_space=pltpu.VMEM)
GRANT = 20 * 2**20
SCALARS = pl.BlockSpec(memory_space=pltpu.SMEM)


def side(kernel, lens, operands, specs, rows, window, width):
    bf = jnp.bfloat16
    wide = min(HEADS_PER_STEP * HD, width)
    return pl.pallas_call(
        kernel,
        grid=(width // wide,),
        in_specs=[SCALARS] + specs,
        out_specs=[columns(rows, wide)] + [columns(window, wide)] * 3,
        out_shape=[jax.ShapeDtypeStruct((rows, width), bf)]
        + [jax.ShapeDtypeStruct((window, width), bf)] * 3,
        scratch_shapes=[pltpu.VMEM((rows, 3 * window // 2), jnp.float32)],
        compiler_params=pltpu.CompilerParams(vmem_limit_bytes=GRANT),
        cost_estimate=cost(rows, 3 * window // 2, width),
        interpret=INTERPRET,
    )(lens, *operands)


def columns(rows, wide, row=0):
    return pl.BlockSpec((rows, wide), lambda h: (row, h))


def assemble_kernel(runs, spreads, group, x, *outs):
    slim = x.shape[2]
    for run in range(runs):
        for spread in range(spreads):
            for core in range(2):
                piece = (run * spreads + spread) * 2 + core
                for j, out in enumerate(outs):
                    left = (core * spreads + spread) * slim
                    out[0, run * group : (run + 1) * group, left : left + slim] = x[
                        piece, j * group : (j + 1) * group, :
                    ]


def assemble(x, runs, spreads, group):
    shape = (1, runs * group, 2 * spreads * x.shape[2])
    return pl.pallas_call(
        functools.partial(assemble_kernel, runs, spreads, group),
        in_specs=[ON_CHIP],
        out_specs=[ON_CHIP] * 3,
        out_shape=[jax.ShapeDtypeStruct(shape, jnp.bfloat16)] * 3,
        compiler_params=pltpu.CompilerParams(vmem_limit_bytes=GRANT),
        name="assemble",
        interpret=INTERPRET,
    )(x)


def shards(vid_q, vid_k, vid_v, vid_dout, aud_q, aud_k, aud_v, aud_dout, aud_len, match):
    frames = lax.axis_size("frame")
    count = lax.axis_size("seq")
    block_here = lax.axis_index("seq")
    core = block_here % 2
    video_rows, width = vid_q.shape[1], vid_q.shape[2]
    audio_rows = aud_q.shape[1]
    half = width // 2
    group = 4 * video_rows // frames
    runs = frames // 4
    spreads = frames // runs
    slim = half // spreads
    f32, bf = jnp.float32, jnp.bfloat16

    pairs = [
        [f * count + 2 * c + k for f in range(frames) for k in range(2)]
        for c in range(count // 2)
    ]

    def pair_exchange(x):
        return lax.all_to_all(
            x, ("frame", "seq"), split_axis=0, concat_axis=0, tiled=True, axis_index_groups=pairs
        )

    def exchange(x):
        return lax.all_to_all(x, "frame", split_axis=0, concat_axis=0, tiled=True)

    def shift(x, by):
        return lax.ppermute(
            x, "seq", [(i, i + by) for i in range(count) if 0 <= i + by < count]
        )

    def swap(x):
        return lax.ppermute(x, "seq", [(i, i ^ 1) for i in range(count)])

    order = jnp.arange(frames, dtype=jnp.int32)
    inverse = jnp.sum(
        jnp.where(match[None, :] == order[:, None], order[None, :], 0), axis=1
    ).astype(jnp.int32)

    packed = jnp.concatenate([vid_q[0], vid_k[0], vid_v[0], vid_dout[0]], axis=0)
    packed = packed.reshape(frames, group, 2, half).transpose(0, 2, 1, 3)
    spread = pair_exchange(packed.reshape(2 * frames, group, half))
    spread = jnp.take(spread.reshape(frames, 2 * group, half), inverse, axis=0, mode="clip")
    video = exchange(spread).reshape(frames * 2 * group, half)

    def halves(x):
        low, high = x[0, :, :half], x[0, :, half:]
        return jnp.where(core == 0, low, high), jnp.where(core == 0, high, low)

    own_k, send_k = halves(aud_k)
    own_v, send_v = halves(aud_v)
    send_q = halves(aud_q)[1]
    send_g = halves(aud_dout)[1]
    sent = jnp.concatenate([send_q, send_k, send_v, send_g], axis=0)
    theirs = swap(sent)
    audio_here = jnp.concatenate(
        [
            own_k,
            theirs[audio_rows : 2 * audio_rows],
            own_v,
            theirs[2 * audio_rows : 3 * audio_rows],
        ],
        axis=0,
    )
    audio_before = shift(audio_here, 2)
    audio_after = shift(audio_here, -2)

    block = 2 * video_rows
    video_here = video[block : 3 * block]
    video_before = shift(video_here, 2)
    video_after = shift(video_here, -2)
    wide = min(HEADS_PER_STEP * HD, half)
    full = pl.BlockSpec((audio_rows, width), lambda h: (0, 0))
    grad_vq, audio_tb, audio_th, audio_ta = side(
        functools.partial(video_kernel, group, count),
        aud_len,
        (video, video, audio_before, audio_here, audio_after),
        [columns(block, wide), columns(block, wide, 3)] + [columns(4 * audio_rows, wide)] * 3,
        block,
        4 * audio_rows,
        half,
    )
    grad_aq, video_tb, video_th, video_ta = side(
        functools.partial(audio_kernel, group, count),
        aud_len,
        (aud_q[0], aud_dout[0], theirs, theirs, video_before, video_here, video_after),
        [full, full, columns(audio_rows, wide), columns(audio_rows, wide, 3)]
        + [columns(2 * block, wide)] * 3,
        2 * audio_rows,
        2 * block,
        half,
    )

    grad_vkv = (
        video_th.astype(f32)
        + shift(video_tb, -2).astype(f32)
        + shift(video_ta, 2).astype(f32)
    ).astype(bf)
    grads = jnp.concatenate([grad_vq, grad_vkv], axis=0)
    grads = grads.reshape(3, runs, 2, group, spreads, slim).transpose(1, 4, 2, 0, 3, 5)
    grads = exchange(grads.reshape(frames, 6 * group, slim))
    grads = jnp.take(grads, match, axis=0, mode="clip")
    grads = pair_exchange(grads.reshape(2 * frames, 3 * group, slim))
    grads = assemble(grads, runs, spreads, group)

    from_after, from_before = shift(audio_tb, -2), shift(audio_ta, 2)
    grad_akv = (audio_th.astype(f32) + from_after.astype(f32) + from_before.astype(f32)).astype(bf)
    mine = (
        grad_aq[:audio_rows],
        grad_akv[:audio_rows],
        grad_akv[2 * audio_rows : 3 * audio_rows],
    )
    back = jnp.concatenate(
        [
            grad_aq[audio_rows:],
            grad_akv[audio_rows : 2 * audio_rows],
            grad_akv[3 * audio_rows :],
        ],
        axis=0,
    )
    back = swap(back)

    def whole(own, other):
        return jnp.where(
            core == 0,
            jnp.concatenate([own, other], axis=1),
            jnp.concatenate([other, own], axis=1),
        )[None]

    outs = [
        whole(mine[j], back[j * audio_rows : (j + 1) * audio_rows]) for j in range(3)
    ]
    return (*grads, *outs)


def solution(mesh):
    tokens = P("frame", "seq", None)
    return jax.shard_map(
        shards,
        mesh=mesh,
        in_specs=(tokens,) * 8 + (P(), P()),
        out_specs=(tokens,) * 6,
        check_vma=False,
    )
```

```python
import functools

import jax
import jax.numpy as jnp
from jax import lax
from jax.experimental import pallas as pl
from jax.experimental.pallas import tpu as pltpu
from jax.sharding import PartitionSpec as P


HD = 128
BAND = 2
NEG_BIG = -1e30
FACTOR = HD ** (-0.5)
HEADS_PER_STEP = 4
INTERPRET = False


def contract(left, right, left_dim, right_dim):
    return lax.dot_general(
        left,
        right,
        (((left_dim,), (right_dim,)), ((), ())),
        preferred_element_type=jnp.float32,
    )


def attend(queries, keys, values, grads, bias):
    total = range(len(queries))
    scores = [contract(queries[h], keys[h], 1, 1) * FACTOR + bias[...] for h in total]
    largest = [jnp.max(scores[h], axis=-1, keepdims=True) for h in total]
    exponent = [jnp.exp(scores[h] - largest[h]) for h in total]
    inverse = [1.0 / jnp.sum(exponent[h], axis=-1, keepdims=True) for h in total]
    weights = [exponent[h] * inverse[h] for h in total]
    half = [weights[h].astype(jnp.bfloat16) for h in total]
    grad_weights = [contract(grads[h], values[h], 1, 1) for h in total]
    delta = [
        jnp.sum(half[h].astype(jnp.float32) * grad_weights[h], axis=-1, keepdims=True)
        for h in total
    ]
    grad_scores = [
        (weights[h] * (grad_weights[h] - delta[h])).astype(jnp.bfloat16) for h in total
    ]
    value_terms = [contract(half[h], grads[h], 0, 0) for h in total]
    grad_query = [contract(grad_scores[h], keys[h], 1, 0) * FACTOR for h in total]
    key_terms = [contract(grad_scores[h], queries[h], 0, 0) * FACTOR for h in total]
    return grad_query, key_terms, value_terms


def windows(refs, part, cols):
    keys = jnp.concatenate([ref[:part, cols] for ref in refs], axis=0)
    values = jnp.concatenate([ref[part:, cols] for ref in refs], axis=0)
    return keys, values


def write(results, spans, dq_ref, term_refs, part):
    for cols, dq, kt, vt in zip(spans, *results, strict=True):
        dq_ref[:, cols] = dq.astype(jnp.bfloat16)
        for place, out in enumerate(term_refs):
            rows = slice(place * part, (place + 1) * part)
            out[:part, cols] = kt[rows].astype(jnp.bfloat16)
            out[part:, cols] = vt[rows].astype(jnp.bfloat16)


def head_spans(wide):
    return [slice(h * HD, (h + 1) * HD) for h in range(wide // HD)]


def video_kernel(group, count, lens, queries, grads, before, here, after, dq_ref, tb, th, ta, bias):
    part = before.shape[0] // 2

    @pl.when(pl.program_id(0) == 0)
    def _():
        video_bias(group, count, lens, part, bias)

    spans = head_spans(dq_ref.shape[1])
    keys, values = zip(*[windows((before, here, after), part, cols) for cols in spans])
    results = attend(
        [queries[:, cols] for cols in spans], keys, values, [grads[:, cols] for cols in spans], bias
    )
    write(results, spans, dq_ref, (tb, th, ta), part)


def video_bias(group, count, lens, part, bias):
    rows, slots = bias.shape[0], part // 2
    frame = lax.axis_index("frame")
    block = lax.axis_index("seq")
    core = lax.rem(block, 2)
    base = block - core
    column = lax.broadcasted_iota(jnp.int32, (1, 3 * part), 1)
    early_row = jnp.full((1, 3 * part), NEG_BIG, jnp.float32)
    late_row = early_row
    for place in range(6):
        offset = 2 * (place // 2) - 2 + (core if place % 2 == 0 else 1 - core)
        time = base + offset
        known = (time >= 0) & (time < count)
        live = lens[frame, jnp.clip(time, 0, count - 1)]
        live = jnp.where(known, live, 0)
        early = jnp.where(jnp.abs(offset) <= BAND, live, 0)
        late = jnp.where(jnp.abs(offset - 1) <= BAND, live, 0)
        first = column >= place * slots
        early_row = jnp.where(first & (column < place * slots + early), 0.0, early_row)
        late_row = jnp.where(first & (column < place * slots + late), 0.0, late_row)
    is_late = (lax.broadcasted_iota(jnp.int32, (rows, 1), 0) // group) % 2
    bias[...] = jnp.where(is_late == 0, early_row, late_row)


def audio_kernel(
    group, count, lens, aud_q, aud_g, their_q, their_g, before, here, after, dq_ref, tb, th, ta, bias
):
    rows, half = aud_q.shape[0], aud_q.shape[1] // 2
    wide = their_q.shape[1]
    part = before.shape[0] // 2
    frame = lax.axis_index("frame")
    block = lax.axis_index("seq")
    core = lax.rem(block, 2)
    base = block - core
    other = base + 1 - core
    column = lax.broadcasted_iota(jnp.int32, (1, 3 * part), 1)
    offset = 2 * (column // part) - 2 + (column // group) % 2
    known = (base + offset >= 0) & (base + offset < count)

    @pl.when(pl.program_id(0) == 0)
    def _():
        for j, own in enumerate((core, 1 - core)):
            seen = known & (jnp.abs(offset - own) <= BAND)
            bias[j * rows : (j + 1) * rows] = jnp.broadcast_to(
                jnp.where(seen, 0.0, NEG_BIG), (rows, 3 * part)
            )

    slot = lax.broadcasted_iota(jnp.int32, (rows, 1), 0)
    live_mine = (slot < lens[frame, block]).astype(jnp.float32)
    live_other = (slot < lens[frame, other]).astype(jnp.float32)

    spans = head_spans(wide)
    queries, grads = [], []
    for head, cols in enumerate(spans):
        start = core * half + pl.program_id(0) * wide + head * HD
        mine = pl.ds(pl.multiple_of(start, HD), HD)
        queries.append(jnp.concatenate([aud_q[:, mine], their_q[:, cols]], axis=0))
        kept = [
            jnp.where(live > 0, rows_of.astype(jnp.float32), 0.0)
            for live, rows_of in ((live_mine, aud_g[:, mine]), (live_other, their_g[:, cols]))
        ]
        grads.append(jnp.concatenate(kept, axis=0).astype(jnp.bfloat16))
    keys, values = zip(*[windows((before, here, after), part, cols) for cols in spans])
    results = attend(queries, keys, values, grads, bias)
    write(results, spans, dq_ref, (tb, th, ta), part)


def cost(rows, keys, width):
    heads_here = width // HD
    return pl.CostEstimate(
        flops=10 * rows * keys * HD * heads_here,
        bytes_accessed=2 * width * (4 * rows + 4 * keys),
        transcendentals=rows * keys * heads_here,
    )


ON_CHIP = pl.BlockSpec(memory_space=pltpu.VMEM)
GRANT = 20 * 2**20
SCALARS = pl.BlockSpec(memory_space=pltpu.SMEM)


def side(kernel, lens, operands, specs, rows, window, width):
    bf = jnp.bfloat16
    wide = min(HEADS_PER_STEP * HD, width)
    return pl.pallas_call(
        kernel,
        grid=(width // wide,),
        in_specs=[SCALARS] + specs,
        out_specs=[columns(rows, wide)] + [columns(window, wide)] * 3,
        out_shape=[jax.ShapeDtypeStruct((rows, width), bf)]
        + [jax.ShapeDtypeStruct((window, width), bf)] * 3,
        scratch_shapes=[pltpu.VMEM((rows, 3 * window // 2), jnp.float32)],
        compiler_params=pltpu.CompilerParams(vmem_limit_bytes=GRANT),
        cost_estimate=cost(rows, 3 * window // 2, width),
        interpret=INTERPRET,
    )(lens, *operands)


def columns(rows, wide, row=0):
    return pl.BlockSpec((rows, wide), lambda h: (row, h))


def place_kernel(spread, index, x, out):
    for frame in range(x.shape[0]):
        if spread:
            out[index[frame]] = x[frame]
        else:
            out[frame] = x[index[frame]]


def place(index, x, spread):
    return pl.pallas_call(
        functools.partial(place_kernel, spread),
        in_specs=[SCALARS, ON_CHIP],
        out_specs=pl.BlockSpec(x.shape, lambda: (0, 0, 0)),
        out_shape=jax.ShapeDtypeStruct(x.shape, x.dtype),
        compiler_params=pltpu.CompilerParams(vmem_limit_bytes=GRANT // 4),
        cost_estimate=pl.CostEstimate(flops=0, bytes_accessed=4 * x.size, transcendentals=0),
        name="place",
        interpret=INTERPRET,
    )(index, x)


def assemble_kernel(runs, spreads, group, x, *outs):
    slim = x.shape[2]
    for run in range(runs):
        for spread in range(spreads):
            for core in range(2):
                piece = (run * spreads + spread) * 2 + core
                for j, out in enumerate(outs):
                    left = (core * spreads + spread) * slim
                    out[0, run * group : (run + 1) * group, left : left + slim] = x[
                        piece, j * group : (j + 1) * group, :
                    ]


def assemble(x, runs, spreads, group):
    shape = (1, runs * group, 2 * spreads * x.shape[2])
    return pl.pallas_call(
        functools.partial(assemble_kernel, runs, spreads, group),
        in_specs=[ON_CHIP],
        out_specs=[ON_CHIP] * 3,
        out_shape=[jax.ShapeDtypeStruct(shape, jnp.bfloat16)] * 3,
        compiler_params=pltpu.CompilerParams(vmem_limit_bytes=GRANT),
        name="assemble",
        interpret=INTERPRET,
    )(x)


def shards(vid_q, vid_k, vid_v, vid_dout, aud_q, aud_k, aud_v, aud_dout, aud_len, match):
    frames = lax.axis_size("frame")
    count = lax.axis_size("seq")
    block_here = lax.axis_index("seq")
    core = block_here % 2
    video_rows, width = vid_q.shape[1], vid_q.shape[2]
    audio_rows = aud_q.shape[1]
    half = width // 2
    group = 4 * video_rows // frames
    runs = frames // 4
    spreads = frames // runs
    slim = half // spreads
    f32, bf = jnp.float32, jnp.bfloat16

    pairs = [
        [f * count + 2 * c + k for f in range(frames) for k in range(2)]
        for c in range(count // 2)
    ]

    def pair_exchange(x):
        return lax.all_to_all(
            x, ("frame", "seq"), split_axis=0, concat_axis=0, tiled=True, axis_index_groups=pairs
        )

    def exchange(x):
        return lax.all_to_all(x, "frame", split_axis=0, concat_axis=0, tiled=True)

    def shift(x, by):
        return lax.ppermute(
            x, "seq", [(i, i + by) for i in range(count) if 0 <= i + by < count]
        )

    def swap(x):
        return lax.ppermute(x, "seq", [(i, i ^ 1) for i in range(count)])

    packed = jnp.concatenate([vid_q[0], vid_k[0], vid_v[0], vid_dout[0]], axis=0)
    packed = packed.reshape(frames, group, 2, half).transpose(0, 2, 1, 3)
    spread = pair_exchange(packed.reshape(2 * frames, group, half))
    spread = place(match, spread.reshape(frames, 2 * group, half), True)
    video = exchange(spread).reshape(frames * 2 * group, half)

    def halves(x):
        low, high = x[0, :, :half], x[0, :, half:]
        return jnp.where(core == 0, low, high), jnp.where(core == 0, high, low)

    own_k, send_k = halves(aud_k)
    own_v, send_v = halves(aud_v)
    send_q = halves(aud_q)[1]
    send_g = halves(aud_dout)[1]
    sent = jnp.concatenate([send_q, send_k, send_v, send_g], axis=0)
    theirs = swap(sent)
    audio_here = jnp.concatenate(
        [
            own_k,
            theirs[audio_rows : 2 * audio_rows],
            own_v,
            theirs[2 * audio_rows : 3 * audio_rows],
        ],
        axis=0,
    )
    audio_before = shift(audio_here, 2)
    audio_after = shift(audio_here, -2)

    block = 2 * video_rows
    video_here = video[block : 3 * block]
    video_before = shift(video_here, 2)
    video_after = shift(video_here, -2)
    wide = min(HEADS_PER_STEP * HD, half)
    full = pl.BlockSpec((audio_rows, width), lambda h: (0, 0))
    grad_vq, audio_tb, audio_th, audio_ta = side(
        functools.partial(video_kernel, group, count),
        aud_len,
        (video, video, audio_before, audio_here, audio_after),
        [columns(block, wide), columns(block, wide, 3)] + [columns(4 * audio_rows, wide)] * 3,
        block,
        4 * audio_rows,
        half,
    )
    grad_aq, video_tb, video_th, video_ta = side(
        functools.partial(audio_kernel, group, count),
        aud_len,
        (aud_q[0], aud_dout[0], theirs, theirs, video_before, video_here, video_after),
        [full, full, columns(audio_rows, wide), columns(audio_rows, wide, 3)]
        + [columns(2 * block, wide)] * 3,
        2 * audio_rows,
        2 * block,
        half,
    )

    from_after, from_before = shift(video_tb, -2), shift(video_ta, 2)
    grad_vkv = (
        video_th.astype(f32) + from_after.astype(f32) + from_before.astype(f32)
    ).astype(bf)
    grads = jnp.concatenate([grad_vq, grad_vkv], axis=0)
    grads = grads.reshape(3, runs, 2, group, spreads, slim).transpose(1, 4, 2, 0, 3, 5)
    grads = exchange(grads.reshape(frames, 6 * group, slim))
    grads = place(match, grads, False)
    grads = pair_exchange(grads.reshape(2 * frames, 3 * group, slim))
    grads = assemble(grads, runs, spreads, group)

    from_after, from_before = shift(audio_tb, -2), shift(audio_ta, 2)
    grad_akv = (audio_th.astype(f32) + from_after.astype(f32) + from_before.astype(f32)).astype(bf)
    mine = (
        grad_aq[:audio_rows],
        grad_akv[:audio_rows],
        grad_akv[2 * audio_rows : 3 * audio_rows],
    )
    back = jnp.concatenate(
        [
            grad_aq[audio_rows:],
            grad_akv[audio_rows : 2 * audio_rows],
            grad_akv[3 * audio_rows :],
        ],
        axis=0,
    )
    back = swap(back)

    def whole(own, other):
        return jnp.where(
            core == 0,
            jnp.concatenate([own, other], axis=1),
            jnp.concatenate([other, own], axis=1),
        )[None]

    outs = [
        whole(mine[j], back[j * audio_rows : (j + 1) * audio_rows]) for j in range(3)
    ]
    return (*grads, *outs)


def solution(mesh):
    tokens = P("frame", "seq", None)
    return jax.shard_map(
        shards,
        mesh=mesh,
        in_specs=(tokens,) * 8 + (P(), P()),
        out_specs=(tokens,) * 6,
        check_vma=False,
    )
```

```python
import functools

import jax
import jax.numpy as jnp
from jax import lax
from jax.experimental import pallas as pl
from jax.experimental.pallas import tpu as pltpu
from jax.sharding import PartitionSpec as P


HD = 128
BAND = 2
NEG_BIG = -1e30
FACTOR = HD ** (-0.5)
INTERPRET = False


def contract(left, right, left_dim, right_dim):
    return lax.dot_general(
        left,
        right,
        (((left_dim,), (right_dim,)), ((), ())),
        preferred_element_type=jnp.float32,
    )


def attend(queries, keys, values, grads, bias):
    total = range(len(queries))
    scores = [contract(queries[h], keys[h], 1, 1) * FACTOR + bias[...] for h in total]
    largest = [jnp.max(scores[h], axis=-1, keepdims=True) for h in total]
    exponent = [jnp.exp(scores[h] - largest[h]) for h in total]
    inverse = [1.0 / jnp.sum(exponent[h], axis=-1, keepdims=True) for h in total]
    weights = [exponent[h] * inverse[h] for h in total]
    half = [weights[h].astype(jnp.bfloat16) for h in total]
    grad_weights = [contract(grads[h], values[h], 1, 1) for h in total]
    delta = [
        jnp.sum(half[h].astype(jnp.float32) * grad_weights[h], axis=-1, keepdims=True)
        for h in total
    ]
    grad_scores = [
        (weights[h] * (grad_weights[h] - delta[h])).astype(jnp.bfloat16) for h in total
    ]
    value_terms = [contract(half[h], grads[h], 0, 0) for h in total]
    grad_query = [contract(grad_scores[h], keys[h], 1, 0) * FACTOR for h in total]
    key_terms = [contract(grad_scores[h], queries[h], 0, 0) * FACTOR for h in total]
    return grad_query, key_terms, value_terms


def windows(refs, part, cols):
    keys = jnp.concatenate([ref[:part, cols] for ref in refs], axis=0)
    values = jnp.concatenate([ref[part:, cols] for ref in refs], axis=0)
    return keys, values


def write(results, spans, dq_ref, term_refs, part):
    for cols, dq, kt, vt in zip(spans, *results, strict=True):
        dq_ref[:, cols] = dq.astype(jnp.bfloat16)
        for place, out in enumerate(term_refs):
            rows = slice(place * part, (place + 1) * part)
            out[:part, cols] = kt[rows].astype(jnp.bfloat16)
            out[part:, cols] = vt[rows].astype(jnp.bfloat16)


def head_spans(wide):
    return [slice(h * HD, (h + 1) * HD) for h in range(wide // HD)]


def video_whole(group, count, lens, video, *refs):
    rows = video.shape[0] // 4
    video_kernel(group, count, lens, video.at[:rows], video.at[3 * rows :], *refs)


def audio_whole(group, count, lens, aud_q, aud_g, theirs, *refs):
    rows = aud_q.shape[0]
    audio_kernel(
        group, count, lens, aud_q, aud_g, theirs.at[:rows], theirs.at[3 * rows :], *refs
    )


def video_kernel(group, count, lens, queries, grads, before, here, after, dq_ref, tb, th, ta, bias):
    part = before.shape[0] // 2

    video_bias(group, count, lens, part, bias)

    spans = head_spans(dq_ref.shape[1])
    keys, values = zip(*[windows((before, here, after), part, cols) for cols in spans])
    results = attend(
        [queries[:, cols] for cols in spans], keys, values, [grads[:, cols] for cols in spans], bias
    )
    write(results, spans, dq_ref, (tb, th, ta), part)


def video_bias(group, count, lens, part, bias):
    rows, slots = bias.shape[0], part // 2
    frame = lax.axis_index("frame")
    block = lax.axis_index("seq")
    core = lax.rem(block, 2)
    base = block - core
    column = lax.broadcasted_iota(jnp.int32, (1, 3 * part), 1)
    early_row = jnp.full((1, 3 * part), NEG_BIG, jnp.float32)
    late_row = early_row
    for place in range(6):
        offset = 2 * (place // 2) - 2 + (core if place % 2 == 0 else 1 - core)
        time = base + offset
        known = (time >= 0) & (time < count)
        live = lens[frame, jnp.clip(time, 0, count - 1)]
        live = jnp.where(known, live, 0)
        early = jnp.where(jnp.abs(offset) <= BAND, live, 0)
        late = jnp.where(jnp.abs(offset - 1) <= BAND, live, 0)
        first = column >= place * slots
        early_row = jnp.where(first & (column < place * slots + early), 0.0, early_row)
        late_row = jnp.where(first & (column < place * slots + late), 0.0, late_row)
    is_late = (lax.broadcasted_iota(jnp.int32, (rows, 1), 0) // group) % 2
    bias[...] = jnp.where(is_late == 0, early_row, late_row)


def audio_kernel(
    group, count, lens, aud_q, aud_g, their_q, their_g, before, here, after, dq_ref, tb, th, ta, bias
):
    rows, half = aud_q.shape[0], aud_q.shape[1] // 2
    wide = their_q.shape[1]
    part = before.shape[0] // 2
    frame = lax.axis_index("frame")
    block = lax.axis_index("seq")
    core = lax.rem(block, 2)
    base = block - core
    other = base + 1 - core
    column = lax.broadcasted_iota(jnp.int32, (1, 3 * part), 1)
    offset = 2 * (column // part) - 2 + (column // group) % 2
    known = (base + offset >= 0) & (base + offset < count)

    for j, own in enumerate((core, 1 - core)):
        seen = known & (jnp.abs(offset - own) <= BAND)
        bias[j * rows : (j + 1) * rows] = jnp.broadcast_to(
            jnp.where(seen, 0.0, NEG_BIG), (rows, 3 * part)
        )

    slot = lax.broadcasted_iota(jnp.int32, (rows, 1), 0)
    live_mine = (slot < lens[frame, block]).astype(jnp.float32)
    live_other = (slot < lens[frame, other]).astype(jnp.float32)

    spans = head_spans(wide)
    queries, grads = [], []
    for head, cols in enumerate(spans):
        start = core * half + head * HD
        mine = pl.ds(pl.multiple_of(start, HD), HD)
        queries.append(jnp.concatenate([aud_q[:, mine], their_q[:, cols]], axis=0))
        kept = [
            jnp.where(live > 0, rows_of.astype(jnp.float32), 0.0)
            for live, rows_of in ((live_mine, aud_g[:, mine]), (live_other, their_g[:, cols]))
        ]
        grads.append(jnp.concatenate(kept, axis=0).astype(jnp.bfloat16))
    keys, values = zip(*[windows((before, here, after), part, cols) for cols in spans])
    results = attend(queries, keys, values, grads, bias)
    write(results, spans, dq_ref, (tb, th, ta), part)


def cost(rows, keys, width):
    heads_here = width // HD
    return pl.CostEstimate(
        flops=10 * rows * keys * HD * heads_here,
        bytes_accessed=2 * width * (4 * rows + 4 * keys),
        transcendentals=rows * keys * heads_here,
    )


ON_CHIP = pl.BlockSpec(memory_space=pltpu.VMEM)
GRANT = 20 * 2**20
SCALARS = pl.BlockSpec(memory_space=pltpu.SMEM)


def side(kernel, lens, operands, rows, window, width):
    bf = jnp.bfloat16
    return pl.pallas_call(
        kernel,
        in_specs=[SCALARS] + [ON_CHIP] * len(operands),
        out_specs=[ON_CHIP] * 4,
        out_shape=[jax.ShapeDtypeStruct((rows, width), bf)]
        + [jax.ShapeDtypeStruct((window, width), bf)] * 3,
        scratch_shapes=[pltpu.VMEM((rows, 3 * window // 2), jnp.float32)],
        compiler_params=pltpu.CompilerParams(vmem_limit_bytes=GRANT),
        cost_estimate=cost(rows, 3 * window // 2, width),
        interpret=INTERPRET,
    )(lens, *operands)


def place_kernel(spread, index, x, out):
    for frame in range(x.shape[0]):
        if spread:
            out[index[frame]] = x[frame]
        else:
            out[frame] = x[index[frame]]


def place(index, x, spread):
    return pl.pallas_call(
        functools.partial(place_kernel, spread),
        in_specs=[SCALARS, ON_CHIP],
        out_specs=pl.BlockSpec(x.shape, lambda: (0, 0, 0)),
        out_shape=jax.ShapeDtypeStruct(x.shape, x.dtype),
        compiler_params=pltpu.CompilerParams(vmem_limit_bytes=GRANT // 4),
        cost_estimate=pl.CostEstimate(flops=0, bytes_accessed=4 * x.size, transcendentals=0),
        name="place",
        interpret=INTERPRET,
    )(index, x)


def assemble_kernel(runs, spreads, group, x, *outs):
    slim = x.shape[2]
    for run in range(runs):
        for spread in range(spreads):
            for core in range(2):
                piece = (run * spreads + spread) * 2 + core
                for j, out in enumerate(outs):
                    left = (core * spreads + spread) * slim
                    out[0, run * group : (run + 1) * group, left : left + slim] = x[
                        piece, j * group : (j + 1) * group, :
                    ]


def assemble(x, runs, spreads, group):
    shape = (1, runs * group, 2 * spreads * x.shape[2])
    return pl.pallas_call(
        functools.partial(assemble_kernel, runs, spreads, group),
        in_specs=[ON_CHIP],
        out_specs=[ON_CHIP] * 3,
        out_shape=[jax.ShapeDtypeStruct(shape, jnp.bfloat16)] * 3,
        compiler_params=pltpu.CompilerParams(vmem_limit_bytes=GRANT),
        name="assemble",
        interpret=INTERPRET,
    )(x)


def shards(vid_q, vid_k, vid_v, vid_dout, aud_q, aud_k, aud_v, aud_dout, aud_len, match):
    frames = lax.axis_size("frame")
    count = lax.axis_size("seq")
    block_here = lax.axis_index("seq")
    core = block_here % 2
    video_rows, width = vid_q.shape[1], vid_q.shape[2]
    audio_rows = aud_q.shape[1]
    half = width // 2
    group = 4 * video_rows // frames
    runs = frames // 4
    spreads = frames // runs
    slim = half // spreads
    f32, bf = jnp.float32, jnp.bfloat16

    pairs = [
        [f * count + 2 * c + k for f in range(frames) for k in range(2)]
        for c in range(count // 2)
    ]

    def pair_exchange(x):
        return lax.all_to_all(
            x, ("frame", "seq"), split_axis=0, concat_axis=0, tiled=True, axis_index_groups=pairs
        )

    def exchange(x):
        return lax.all_to_all(x, "frame", split_axis=0, concat_axis=0, tiled=True)

    def shift(x, by):
        return lax.ppermute(
            x, "seq", [(i, i + by) for i in range(count) if 0 <= i + by < count]
        )

    def swap(x):
        return lax.ppermute(x, "seq", [(i, i ^ 1) for i in range(count)])

    packed = jnp.concatenate([vid_q[0], vid_k[0], vid_v[0], vid_dout[0]], axis=0)
    packed = packed.reshape(frames, group, 2, half).transpose(0, 2, 1, 3)
    spread = pair_exchange(packed.reshape(2 * frames, group, half))
    spread = place(match, spread.reshape(frames, 2 * group, half), True)
    video = exchange(spread).reshape(frames * 2 * group, half)

    def halves(x):
        low, high = x[0, :, :half], x[0, :, half:]
        return jnp.where(core == 0, low, high), jnp.where(core == 0, high, low)

    own_k, send_k = halves(aud_k)
    own_v, send_v = halves(aud_v)
    send_q = halves(aud_q)[1]
    send_g = halves(aud_dout)[1]
    sent = jnp.concatenate([send_q, send_k, send_v, send_g], axis=0)
    theirs = swap(sent)
    audio_here = jnp.concatenate(
        [
            own_k,
            theirs[audio_rows : 2 * audio_rows],
            own_v,
            theirs[2 * audio_rows : 3 * audio_rows],
        ],
        axis=0,
    )
    audio_before = shift(audio_here, 2)
    audio_after = shift(audio_here, -2)

    block = 2 * video_rows
    video_here = video[block : 3 * block]
    video_before = shift(video_here, 2)
    video_after = shift(video_here, -2)
    grad_vq, audio_tb, audio_th, audio_ta = side(
        functools.partial(video_whole, group, count),
        aud_len,
        (video, audio_before, audio_here, audio_after),
        block,
        4 * audio_rows,
        half,
    )
    grad_aq, video_tb, video_th, video_ta = side(
        functools.partial(audio_whole, group, count),
        aud_len,
        (aud_q[0], aud_dout[0], theirs, video_before, video_here, video_after),
        2 * audio_rows,
        2 * block,
        half,
    )

    from_after, from_before = shift(video_tb, -2), shift(video_ta, 2)
    grad_vkv = (
        video_th.astype(f32) + from_after.astype(f32) + from_before.astype(f32)
    ).astype(bf)
    grads = jnp.concatenate([grad_vq, grad_vkv], axis=0)
    grads = grads.reshape(3, runs, 2, group, spreads, slim).transpose(1, 4, 2, 0, 3, 5)
    grads = exchange(grads.reshape(frames, 6 * group, slim))
    grads = place(match, grads, False)
    grads = pair_exchange(grads.reshape(2 * frames, 3 * group, slim))
    grads = assemble(grads, runs, spreads, group)

    from_after, from_before = shift(audio_tb, -2), shift(audio_ta, 2)
    grad_akv = (
        audio_th.astype(f32) + from_after.astype(f32) + from_before.astype(f32)
    ).astype(bf)
    mine = (
        grad_aq[:audio_rows],
        grad_akv[:audio_rows],
        grad_akv[2 * audio_rows : 3 * audio_rows],
    )
    back = jnp.concatenate(
        [
            grad_aq[audio_rows:],
            grad_akv[audio_rows : 2 * audio_rows],
            grad_akv[3 * audio_rows :],
        ],
        axis=0,
    )
    back = swap(back)

    def whole(own, other):
        return jnp.where(
            core == 0,
            jnp.concatenate([own, other], axis=1),
            jnp.concatenate([other, own], axis=1),
        )[None]

    outs = [
        whole(mine[j], back[j * audio_rows : (j + 1) * audio_rows]) for j in range(3)
    ]
    return (*grads, *outs)


def solution(mesh):
    tokens = P("frame", "seq", None)
    return jax.shard_map(
        shards,
        mesh=mesh,
        in_specs=(tokens,) * 8 + (P(), P()),
        out_specs=(tokens,) * 6,
        check_vma=False,
    )
```

```python
import functools

import jax
import jax.numpy as jnp
from jax import lax
from jax.experimental import pallas as pl
from jax.experimental.pallas import tpu as pltpu
from jax.sharding import PartitionSpec as P


HD = 128
BAND = 2
NEG_BIG = -1e30
FACTOR = HD ** (-0.5)
INTERPRET = False


def contract(left, right, left_dim, right_dim):
    return lax.dot_general(
        left,
        right,
        (((left_dim,), (right_dim,)), ((), ())),
        preferred_element_type=jnp.float32,
    )


def attend(queries, keys, values, grads, bias):
    total = range(len(queries))
    scores = [contract(queries[h], keys[h], 1, 1) * FACTOR + bias[...] for h in total]
    largest = [jnp.max(scores[h], axis=-1, keepdims=True) for h in total]
    exponent = [jnp.exp(scores[h] - largest[h]) for h in total]
    inverse = [1.0 / jnp.sum(exponent[h], axis=-1, keepdims=True) for h in total]
    weights = [exponent[h] * inverse[h] for h in total]
    half = [weights[h].astype(jnp.bfloat16) for h in total]
    grad_weights = [contract(grads[h], values[h], 1, 1) for h in total]
    delta = [
        jnp.sum(half[h].astype(jnp.float32) * grad_weights[h], axis=-1, keepdims=True)
        for h in total
    ]
    grad_scores = [
        (weights[h] * (grad_weights[h] - delta[h])).astype(jnp.bfloat16) for h in total
    ]
    grad_query = [contract(grad_scores[h], keys[h], 1, 0) * FACTOR for h in total]
    return grad_query, half, grad_scores, (largest, inverse, delta)


def terms(queries, grads, half, grad_scores):
    total = range(len(queries))
    value_terms = [contract(half[h], grads[h], 0, 0) for h in total]
    key_terms = [contract(grad_scores[h], queries[h], 0, 0) * FACTOR for h in total]
    return key_terms, value_terms


def split_stats(value):
    high = value.astype(jnp.bfloat16)
    rest = value - high.astype(jnp.float32)
    middle = rest.astype(jnp.bfloat16)
    low = (rest - middle.astype(jnp.float32)).astype(jnp.bfloat16)
    return high, middle, low


def windows(refs, part, cols):
    keys = jnp.concatenate([ref[:part, cols] for ref in refs], axis=0)
    values = jnp.concatenate([ref[part:, cols] for ref in refs], axis=0)
    return keys, values


def head_spans(wide):
    return [slice(h * HD, (h + 1) * HD) for h in range(wide // HD)]


STAT_ROWS = 8


def video_kernel(group, count, lens, video, before, here, after, dq_ref, out, bias):
    rows = video.shape[0] // 4
    part = before.shape[0] // 2
    video_bias(group, count, lens, part, bias)
    spans = head_spans(dq_ref.shape[1])
    keys, values = zip(*[windows((before, here, after), part, cols) for cols in spans])
    queries = [video[:rows, cols] for cols in spans]
    grads = [video[3 * rows :, cols] for cols in spans]
    grad_query, _, _, stats = attend(queries, keys, values, grads, bias)
    lane = lax.broadcasted_iota(jnp.int32, (rows, HD), 1)
    table = jnp.zeros((rows, HD), jnp.float32)
    for j, stat in enumerate(stats):
        for h, value in enumerate(stat):
            table = jnp.where(lane == j * len(spans) + h, value, table)
    for cols, dq in zip(spans, grad_query, strict=True):
        dq_ref[:, cols] = dq.astype(jnp.bfloat16)
    out[:rows] = video[:rows]
    out[rows : 2 * rows] = video[3 * rows :]
    for j, piece in enumerate(split_stats(table)):
        top = 2 * rows + j * STAT_ROWS
        for k in range(rows // STAT_ROWS):
            out[top : top + STAT_ROWS, k * HD : (k + 1) * HD] = piece[
                k * STAT_ROWS : (k + 1) * STAT_ROWS
            ]


def terms_kernel(group, count, lens, before, here, after, audio, dkv_ref, bias):
    rows = (before.shape[0] - 3 * STAT_ROWS) // 2
    part = audio.shape[0] // 2
    slots = part // 2
    frame = lax.axis_index("frame")
    block = lax.axis_index("seq")
    core = lax.rem(block, 2)
    base = block - core
    place = lax.broadcasted_iota(jnp.int32, (3 * rows, 1), 0)
    offset = 2 * (place // rows) - 2 + (place // group) % 2
    known = (base + offset >= 0) & (base + offset < count)
    column = lax.broadcasted_iota(jnp.int32, (1, part), 1)
    mine = column < slots
    slot = jnp.where(mine, column, column - slots)
    live = slot < jnp.where(mine, lens[frame, block], lens[frame, base + 1 - core])
    own = jnp.where(mine, core, 1 - core)
    near = jnp.where(known, 0.0, NEG_BIG) + jnp.where(live, 0.0, NEG_BIG)
    bias[...] = jnp.where(jnp.abs(offset - own) <= BAND, near, NEG_BIG)
    refs = (before, here, after)
    spans = head_spans(dkv_ref.shape[1])
    total = range(len(spans))
    queries = [jnp.concatenate([ref[:rows, cols] for ref in refs], axis=0) for cols in spans]
    grads = [
        jnp.concatenate([ref[rows : 2 * rows, cols] for ref in refs], axis=0) for cols in spans
    ]
    tables = []
    for ref in refs:
        value = 0.0
        for j in range(3):
            top = 2 * rows + j * STAT_ROWS
            wide = ref[top : top + STAT_ROWS, : rows // STAT_ROWS * HD].astype(jnp.float32)
            value = value + wide
        for k in range(rows // STAT_ROWS):
            tables.append(value[:, k * HD : (k + 1) * HD])
    table = jnp.concatenate(tables, axis=0)
    largest, inverse, delta = [
        [table[:, j * len(spans) + h : j * len(spans) + h + 1] for h in total] for j in range(3)
    ]
    scores = [contract(queries[h], audio[:part, spans[h]], 1, 1) * FACTOR + bias[...] for h in total]
    weights = [jnp.exp(scores[h] - largest[h]) * inverse[h] for h in total]
    half = [weights[h].astype(jnp.bfloat16) for h in total]
    grad_weights = [contract(grads[h], audio[part:, spans[h]], 1, 1) for h in total]
    grad_scores = [
        (weights[h] * (grad_weights[h] - delta[h])).astype(jnp.bfloat16) for h in total
    ]
    key_terms, value_terms = terms(queries, grads, half, grad_scores)
    for h in total:
        dkv_ref[:part, spans[h]] = key_terms[h].astype(jnp.bfloat16)
        dkv_ref[part:, spans[h]] = value_terms[h].astype(jnp.bfloat16)


def video_bias(group, count, lens, part, bias):
    rows, slots = bias.shape[0], part // 2
    frame = lax.axis_index("frame")
    block = lax.axis_index("seq")
    core = lax.rem(block, 2)
    base = block - core
    column = lax.broadcasted_iota(jnp.int32, (1, 3 * part), 1)
    early_row = jnp.full((1, 3 * part), NEG_BIG, jnp.float32)
    late_row = early_row
    for place in range(6):
        offset = 2 * (place // 2) - 2 + (core if place % 2 == 0 else 1 - core)
        time = base + offset
        known = (time >= 0) & (time < count)
        live = lens[frame, jnp.clip(time, 0, count - 1)]
        live = jnp.where(known, live, 0)
        early = jnp.where(jnp.abs(offset) <= BAND, live, 0)
        late = jnp.where(jnp.abs(offset - 1) <= BAND, live, 0)
        first = column >= place * slots
        early_row = jnp.where(first & (column < place * slots + early), 0.0, early_row)
        late_row = jnp.where(first & (column < place * slots + late), 0.0, late_row)
    is_late = (lax.broadcasted_iota(jnp.int32, (rows, 1), 0) // group) % 2
    bias[...] = jnp.where(is_late == 0, early_row, late_row)


def audio_whole(group, count, lens, aud_q, aud_g, theirs, *refs):
    rows = aud_q.shape[0]
    audio_kernel(
        group, count, lens, aud_q, aud_g, theirs.at[:rows], theirs.at[3 * rows :], *refs
    )


def audio_kernel(
    group, count, lens, aud_q, aud_g, their_q, their_g, before, here, after, dq_ref, tb, th, ta, bias
):
    rows, half = aud_q.shape[0], aud_q.shape[1] // 2
    wide = their_q.shape[1]
    part = before.shape[0] // 2
    frame = lax.axis_index("frame")
    block = lax.axis_index("seq")
    core = lax.rem(block, 2)
    base = block - core
    other = base + 1 - core
    column = lax.broadcasted_iota(jnp.int32, (1, 3 * part), 1)
    offset = 2 * (column // part) - 2 + (column // group) % 2
    known = (base + offset >= 0) & (base + offset < count)

    for j, own in enumerate((core, 1 - core)):
        seen = known & (jnp.abs(offset - own) <= BAND)
        bias[j * rows : (j + 1) * rows] = jnp.broadcast_to(
            jnp.where(seen, 0.0, NEG_BIG), (rows, 3 * part)
        )

    slot = lax.broadcasted_iota(jnp.int32, (rows, 1), 0)
    live_mine = (slot < lens[frame, block]).astype(jnp.float32)
    live_other = (slot < lens[frame, other]).astype(jnp.float32)

    spans = head_spans(wide)
    queries, grads = [], []
    for head, cols in enumerate(spans):
        start = core * half + head * HD
        mine = pl.ds(pl.multiple_of(start, HD), HD)
        queries.append(jnp.concatenate([aud_q[:, mine], their_q[:, cols]], axis=0))
        kept = [
            jnp.where(live > 0, rows_of.astype(jnp.float32), 0.0)
            for live, rows_of in ((live_mine, aud_g[:, mine]), (live_other, their_g[:, cols]))
        ]
        grads.append(jnp.concatenate(kept, axis=0).astype(jnp.bfloat16))
    keys, values = zip(*[windows((before, here, after), part, cols) for cols in spans])
    grad_query, weights, grad_scores, _ = attend(queries, keys, values, grads, bias)
    key_terms, value_terms = terms(queries, grads, weights, grad_scores)
    for h, cols in enumerate(spans):
        dq_ref[:, cols] = grad_query[h].astype(jnp.bfloat16)
        for place, out in enumerate((tb, th, ta)):
            span = slice(place * part, (place + 1) * part)
            out[:part, cols] = key_terms[h][span].astype(jnp.bfloat16)
            out[part:, cols] = value_terms[h][span].astype(jnp.bfloat16)


def cost(rows, keys, width):
    heads_here = width // HD
    return pl.CostEstimate(
        flops=10 * rows * keys * HD * heads_here,
        bytes_accessed=2 * width * (4 * rows + 4 * keys),
        transcendentals=rows * keys * heads_here,
    )


ON_CHIP = pl.BlockSpec(memory_space=pltpu.VMEM)
GRANT = 20 * 2**20
SCALARS = pl.BlockSpec(memory_space=pltpu.SMEM)


def side(kernel, lens, operands, outs, scores):
    width = outs[0][1]
    return pl.pallas_call(
        kernel,
        in_specs=[SCALARS] + [ON_CHIP] * len(operands),
        out_specs=[ON_CHIP] * len(outs),
        out_shape=[jax.ShapeDtypeStruct(shape, jnp.bfloat16) for shape in outs],
        scratch_shapes=[pltpu.VMEM(scores, jnp.float32)],
        compiler_params=pltpu.CompilerParams(vmem_limit_bytes=GRANT),
        cost_estimate=cost(*scores, width),
        interpret=INTERPRET,
    )(lens, *operands)


def gather_kernel(runs, spreads, group, dq, th, t1, t2, out):
    rows, slim = dq.shape[0], out.shape[2]
    core = lax.rem(lax.axis_index("seq"), 2)
    for run in range(runs):
        here = slice(run * 2 * group, (run + 1) * 2 * group)
        values = [dq[here]]
        for start in (0, rows):
            there = slice(start + here.start, start + here.stop)
            total = th[there].astype(jnp.float32) + t1[there].astype(jnp.float32)
            values.append((total + t2[there].astype(jnp.float32)).astype(jnp.bfloat16))
        for spread in range(spreads):
            cols = slice(spread * slim, (spread + 1) * slim)
            for late in range(2):
                for j, value in enumerate(values):
                    other = core if late == 0 else 1 - core
                    left = pl.multiple_of((other * 3 + j) * group, group)
                    out[run * spreads + spread, pl.ds(left, group)] = value[
                        late * group : (late + 1) * group, cols
                    ]


def gather(dq, th, t1, t2, runs, spreads, group):
    return pl.pallas_call(
        functools.partial(gather_kernel, runs, spreads, group),
        in_specs=[ON_CHIP] * 4,
        out_specs=ON_CHIP,
        out_shape=jax.ShapeDtypeStruct(
            (runs * spreads, 6 * group, dq.shape[1] // spreads), jnp.bfloat16
        ),
        compiler_params=pltpu.CompilerParams(vmem_limit_bytes=GRANT // 4),
        cost_estimate=pl.CostEstimate(flops=0, bytes_accessed=16 * dq.size, transcendentals=0),
        name="gather",
        interpret=INTERPRET,
    )(dq, th, t1, t2)


def place_kernel(spread, index, x, out):
    for frame in range(x.shape[0]):
        if spread:
            out[index[frame]] = x[frame]
        else:
            out[frame] = x[index[frame]]


def place(index, x, spread):
    return pl.pallas_call(
        functools.partial(place_kernel, spread),
        in_specs=[SCALARS, ON_CHIP],
        out_specs=ON_CHIP,
        out_shape=jax.ShapeDtypeStruct(x.shape, x.dtype),
        compiler_params=pltpu.CompilerParams(vmem_limit_bytes=GRANT // 4),
        cost_estimate=pl.CostEstimate(flops=0, bytes_accessed=4 * x.size, transcendentals=0),
        name="place",
        interpret=INTERPRET,
    )(index, x)


def assemble_kernel(runs, spreads, group, x, other, *outs):
    slim = x.shape[2]
    half = spreads * slim
    core = lax.rem(lax.axis_index("seq"), 2)
    for run in range(runs):
        rows = slice(run * group, (run + 1) * group)
        for spread in range(spreads):
            piece = run * spreads + spread
            for source, start in ((x, core * half), (other, (1 - core) * half)):
                cols = pl.ds(pl.multiple_of(start + spread * slim, HD), slim)
                for j, out in enumerate(outs):
                    out[0, rows, cols] = source[piece, j * group : (j + 1) * group]


def assemble(x, other, runs, spreads, group):
    shape = (1, runs * group, 2 * spreads * x.shape[2])
    return pl.pallas_call(
        functools.partial(assemble_kernel, runs, spreads, group),
        in_specs=[ON_CHIP] * 2,
        out_specs=[ON_CHIP] * 3,
        out_shape=[jax.ShapeDtypeStruct(shape, jnp.bfloat16)] * 3,
        compiler_params=pltpu.CompilerParams(vmem_limit_bytes=GRANT // 4),
        name="assemble",
        interpret=INTERPRET,
    )(x, other)


def shards(vid_q, vid_k, vid_v, vid_dout, aud_q, aud_k, aud_v, aud_dout, aud_len, match):
    frames = lax.axis_size("frame")
    count = lax.axis_size("seq")
    block_here = lax.axis_index("seq")
    core = block_here % 2
    video_rows, width = vid_q.shape[1], vid_q.shape[2]
    audio_rows = aud_q.shape[1]
    half = width // 2
    group = 4 * video_rows // frames
    runs = frames // 4
    spreads = frames // runs

    pairs = [
        [f * count + 2 * c + k for f in range(frames) for k in range(2)]
        for c in range(count // 2)
    ]

    def pair_exchange(x):
        return lax.all_to_all(
            x, ("frame", "seq"), split_axis=0, concat_axis=0, tiled=True, axis_index_groups=pairs
        )

    def exchange(x):
        return lax.all_to_all(x, "frame", split_axis=0, concat_axis=0, tiled=True)

    def shift(x, by):
        return lax.ppermute(
            x, "seq", [(i, i + by) for i in range(count) if 0 <= i + by < count]
        )

    def swap(x):
        return lax.ppermute(x, "seq", [(i, i ^ 1) for i in range(count)])

    packed = jnp.concatenate([vid_q[0], vid_k[0], vid_v[0], vid_dout[0]], axis=0)
    packed = packed.reshape(frames, group, 2, half).transpose(0, 2, 1, 3)
    spread = pair_exchange(packed.reshape(2 * frames, group, half))
    spread = place(match, spread.reshape(frames, 2 * group, half), True)
    video = exchange(spread).reshape(frames * 2 * group, half)

    def halves(x):
        low, high = x[0, :, :half], x[0, :, half:]
        return jnp.where(core == 0, low, high), jnp.where(core == 0, high, low)

    own_k, send_k = halves(aud_k)
    own_v, send_v = halves(aud_v)
    send_q = halves(aud_q)[1]
    send_g = halves(aud_dout)[1]
    sent = jnp.concatenate([send_q, send_k, send_v, send_g], axis=0)
    theirs = swap(sent)
    audio_here = jnp.concatenate(
        [
            own_k,
            theirs[audio_rows : 2 * audio_rows],
            own_v,
            theirs[2 * audio_rows : 3 * audio_rows],
        ],
        axis=0,
    )
    audio_before = shift(audio_here, 2)
    audio_after = shift(audio_here, -2)

    block = 2 * video_rows
    video_here = video[block : 3 * block]
    video_before = shift(video_here, 2)
    video_after = shift(video_here, -2)
    grad_vq, shared = side(
        functools.partial(video_kernel, group, count),
        aud_len,
        (video, audio_before, audio_here, audio_after),
        [(block, half), (2 * block + 3 * STAT_ROWS, half)],
        (block, 6 * audio_rows),
    )
    grad_aq, video_tb, video_th, video_ta = side(
        functools.partial(audio_whole, group, count),
        aud_len,
        (aud_q[0], aud_dout[0], theirs, video_before, video_here, video_after),
        [(2 * audio_rows, half)] + [(2 * block, half)] * 3,
        (2 * audio_rows, 3 * block),
    )

    from_after, from_before = shift(video_tb, -2), shift(video_ta, 2)
    grads = gather(grad_vq, video_th, from_after, from_before, runs, spreads, group)
    grads = exchange(grads)
    grads = place(match, grads, False)
    grads = exchange(grads)
    other = swap(grads[:, 3 * group :])
    grads = assemble(grads, other, runs, spreads, group)

    shared_before, shared_after = shift(shared, 2), shift(shared, -2)
    (grad_akv,) = side(
        functools.partial(terms_kernel, group, count),
        aud_len,
        (shared_before, shared, shared_after, audio_here),
        [(4 * audio_rows, half)],
        (3 * block, 2 * audio_rows),
    )
    mine = (
        grad_aq[:audio_rows],
        grad_akv[:audio_rows],
        grad_akv[2 * audio_rows : 3 * audio_rows],
    )
    back = jnp.concatenate(
        [
            grad_aq[audio_rows:],
            grad_akv[audio_rows : 2 * audio_rows],
            grad_akv[3 * audio_rows :],
        ],
        axis=0,
    )
    back = swap(back)

    def whole(own, other):
        return jnp.where(
            core == 0,
            jnp.concatenate([own, other], axis=1),
            jnp.concatenate([other, own], axis=1),
        )[None]

    outs = [
        whole(mine[j], back[j * audio_rows : (j + 1) * audio_rows]) for j in range(3)
    ]
    return (*grads, *outs)


def solution(mesh):
    tokens = P("frame", "seq", None)
    return jax.shard_map(
        shards,
        mesh=mesh,
        in_specs=(tokens,) * 8 + (P(), P()),
        out_specs=(tokens,) * 6,
        check_vma=False,
    )
```

```python
import functools

import jax
import jax.numpy as jnp
from jax import lax
from jax.experimental import pallas as pl
from jax.experimental.pallas import tpu as pltpu
from jax.sharding import PartitionSpec as P


HD = 128
BAND = 2
NEG_BIG = -1e30
FACTOR = HD ** (-0.5)
INTERPRET = False


def contract(left, right, left_dim, right_dim):
    return lax.dot_general(
        left,
        right,
        (((left_dim,), (right_dim,)), ((), ())),
        preferred_element_type=jnp.float32,
    )


def attend(queries, keys, values, grads, bias):
    total = range(len(queries))
    scores = [contract(queries[h], keys[h], 1, 1) * FACTOR + bias[...] for h in total]
    largest = [jnp.max(scores[h], axis=-1, keepdims=True) for h in total]
    exponent = [jnp.exp(scores[h] - largest[h]) for h in total]
    inverse = [1.0 / jnp.sum(exponent[h], axis=-1, keepdims=True) for h in total]
    weights = [exponent[h] * inverse[h] for h in total]
    half = [weights[h].astype(jnp.bfloat16) for h in total]
    grad_weights = [contract(grads[h], values[h], 1, 1) for h in total]
    delta = [
        jnp.sum(half[h].astype(jnp.float32) * grad_weights[h], axis=-1, keepdims=True)
        for h in total
    ]
    grad_scores = [
        (weights[h] * (grad_weights[h] - delta[h])).astype(jnp.bfloat16) for h in total
    ]
    grad_query = [contract(grad_scores[h], keys[h], 1, 0) * FACTOR for h in total]
    return grad_query, half, grad_scores, (largest, inverse, delta)


def terms(queries, grads, half, grad_scores):
    total = range(len(queries))
    value_terms = [contract(half[h], grads[h], 0, 0) for h in total]
    key_terms = [contract(grad_scores[h], queries[h], 0, 0) * FACTOR for h in total]
    return key_terms, value_terms


def split_stats(value):
    high = value.astype(jnp.bfloat16)
    rest = value - high.astype(jnp.float32)
    middle = rest.astype(jnp.bfloat16)
    low = (rest - middle.astype(jnp.float32)).astype(jnp.bfloat16)
    return high, middle, low


def windows(refs, part, cols):
    keys = jnp.concatenate([ref[:part, cols] for ref in refs], axis=0)
    values = jnp.concatenate([ref[part:, cols] for ref in refs], axis=0)
    return keys, values


def head_spans(wide):
    return [slice(h * HD, (h + 1) * HD) for h in range(wide // HD)]


STAT_ROWS = 8


def video_kernel(group, count, lens, video, before, here, after, dq_ref, out, bias):
    rows = video.shape[0] // 4
    part = before.shape[0] // 2
    video_bias(group, count, lens, part, bias)
    spans = head_spans(dq_ref.shape[1])
    keys, values = zip(*[windows((before, here, after), part, cols) for cols in spans])
    queries = [video[:rows, cols] for cols in spans]
    grads = [video[3 * rows :, cols] for cols in spans]
    grad_query, _, _, stats = attend(queries, keys, values, grads, bias)
    lane = lax.broadcasted_iota(jnp.int32, (rows, HD), 1)
    table = jnp.zeros((rows, HD), jnp.float32)
    for j, stat in enumerate(stats):
        for h, value in enumerate(stat):
            table = jnp.where(lane == j * len(spans) + h, value, table)
    for cols, dq in zip(spans, grad_query, strict=True):
        dq_ref[:, cols] = dq.astype(jnp.bfloat16)
    out[:rows] = video[:rows]
    out[rows : 2 * rows] = video[3 * rows :]
    for j, piece in enumerate(split_stats(table)):
        top = 2 * rows + j * STAT_ROWS
        for k in range(rows // STAT_ROWS):
            out[top : top + STAT_ROWS, k * HD : (k + 1) * HD] = piece[
                k * STAT_ROWS : (k + 1) * STAT_ROWS
            ]


def terms_kernel(group, count, lens, before, here, after, audio, dkv_ref, bias):
    rows = (before.shape[0] - 3 * STAT_ROWS) // 2
    part = audio.shape[0] // 2
    slots = part // 2
    frame = lax.axis_index("frame")
    block = lax.axis_index("seq")
    core = lax.rem(block, 2)
    base = block - core
    place = lax.broadcasted_iota(jnp.int32, (3 * rows, 1), 0)
    offset = 2 * (place // rows) - 2 + (place // group) % 2
    known = (base + offset >= 0) & (base + offset < count)
    column = lax.broadcasted_iota(jnp.int32, (1, part), 1)
    mine = column < slots
    slot = jnp.where(mine, column, column - slots)
    live = slot < jnp.where(mine, lens[frame, block], lens[frame, base + 1 - core])
    own = jnp.where(mine, core, 1 - core)
    near = jnp.where(known, 0.0, NEG_BIG) + jnp.where(live, 0.0, NEG_BIG)
    bias[...] = jnp.where(jnp.abs(offset - own) <= BAND, near, NEG_BIG)
    refs = (before, here, after)
    spans = head_spans(dkv_ref.shape[1])
    total = range(len(spans))
    queries = [jnp.concatenate([ref[:rows, cols] for ref in refs], axis=0) for cols in spans]
    grads = [
        jnp.concatenate([ref[rows : 2 * rows, cols] for ref in refs], axis=0) for cols in spans
    ]
    tables = []
    for ref in refs:
        value = 0.0
        for j in range(3):
            top = 2 * rows + j * STAT_ROWS
            wide = ref[top : top + STAT_ROWS, : rows // STAT_ROWS * HD].astype(jnp.float32)
            value = value + wide
        for k in range(rows // STAT_ROWS):
            tables.append(value[:, k * HD : (k + 1) * HD])
    table = jnp.concatenate(tables, axis=0)
    largest, inverse, delta = [
        [table[:, j * len(spans) + h : j * len(spans) + h + 1] for h in total] for j in range(3)
    ]
    scores = [contract(queries[h], audio[:part, spans[h]], 1, 1) * FACTOR + bias[...] for h in total]
    weights = [jnp.exp(scores[h] - largest[h]) * inverse[h] for h in total]
    half = [weights[h].astype(jnp.bfloat16) for h in total]
    grad_weights = [contract(grads[h], audio[part:, spans[h]], 1, 1) for h in total]
    grad_scores = [
        (weights[h] * (grad_weights[h] - delta[h])).astype(jnp.bfloat16) for h in total
    ]
    key_terms, value_terms = terms(queries, grads, half, grad_scores)
    for h in total:
        dkv_ref[:part, spans[h]] = key_terms[h].astype(jnp.bfloat16)
        dkv_ref[part:, spans[h]] = value_terms[h].astype(jnp.bfloat16)


def video_bias(group, count, lens, part, bias):
    rows, slots = bias.shape[0], part // 2
    frame = lax.axis_index("frame")
    block = lax.axis_index("seq")
    core = lax.rem(block, 2)
    base = block - core
    column = lax.broadcasted_iota(jnp.int32, (1, 3 * part), 1)
    early_row = jnp.full((1, 3 * part), NEG_BIG, jnp.float32)
    late_row = early_row
    for place in range(6):
        offset = 2 * (place // 2) - 2 + (core if place % 2 == 0 else 1 - core)
        time = base + offset
        known = (time >= 0) & (time < count)
        live = lens[frame, jnp.clip(time, 0, count - 1)]
        live = jnp.where(known, live, 0)
        early = jnp.where(jnp.abs(offset) <= BAND, live, 0)
        late = jnp.where(jnp.abs(offset - 1) <= BAND, live, 0)
        first = column >= place * slots
        early_row = jnp.where(first & (column < place * slots + early), 0.0, early_row)
        late_row = jnp.where(first & (column < place * slots + late), 0.0, late_row)
    is_late = (lax.broadcasted_iota(jnp.int32, (rows, 1), 0) // group) % 2
    bias[...] = jnp.where(is_late == 0, early_row, late_row)


def audio_whole(group, count, lens, aud_q, aud_g, theirs, *refs):
    rows = aud_q.shape[0]
    audio_kernel(
        group, count, lens, aud_q, aud_g, theirs.at[:rows], theirs.at[3 * rows :], *refs
    )


def audio_kernel(
    group, count, lens, aud_q, aud_g, their_q, their_g, before, here, after, dq_ref, tb, th, ta, bias
):
    rows, half = aud_q.shape[0], aud_q.shape[1] // 2
    wide = their_q.shape[1]
    part = before.shape[0] // 2
    frame = lax.axis_index("frame")
    block = lax.axis_index("seq")
    core = lax.rem(block, 2)
    base = block - core
    other = base + 1 - core
    column = lax.broadcasted_iota(jnp.int32, (1, 3 * part), 1)
    offset = 2 * (column // part) - 2 + (column // group) % 2
    known = (base + offset >= 0) & (base + offset < count)

    for j, own in enumerate((core, 1 - core)):
        seen = known & (jnp.abs(offset - own) <= BAND)
        bias[j * rows : (j + 1) * rows] = jnp.broadcast_to(
            jnp.where(seen, 0.0, NEG_BIG), (rows, 3 * part)
        )

    slot = lax.broadcasted_iota(jnp.int32, (rows, 1), 0)
    live_mine = (slot < lens[frame, block]).astype(jnp.float32)
    live_other = (slot < lens[frame, other]).astype(jnp.float32)

    spans = head_spans(wide)
    queries, grads = [], []
    for head, cols in enumerate(spans):
        start = core * half + head * HD
        mine = pl.ds(pl.multiple_of(start, HD), HD)
        queries.append(jnp.concatenate([aud_q[:, mine], their_q[:, cols]], axis=0))
        kept = [
            jnp.where(live > 0, rows_of.astype(jnp.float32), 0.0)
            for live, rows_of in ((live_mine, aud_g[:, mine]), (live_other, their_g[:, cols]))
        ]
        grads.append(jnp.concatenate(kept, axis=0).astype(jnp.bfloat16))
    keys, values = zip(*[windows((before, here, after), part, cols) for cols in spans])
    grad_query, weights, grad_scores, _ = attend(queries, keys, values, grads, bias)
    key_terms, value_terms = terms(queries, grads, weights, grad_scores)
    for h, cols in enumerate(spans):
        dq_ref[:, cols] = grad_query[h].astype(jnp.bfloat16)
        for place, out in enumerate((tb, th, ta)):
            span = slice(place * part, (place + 1) * part)
            out[:part, cols] = key_terms[h][span].astype(jnp.bfloat16)
            out[part:, cols] = value_terms[h][span].astype(jnp.bfloat16)


def cost(rows, keys, width):
    heads_here = width // HD
    return pl.CostEstimate(
        flops=10 * rows * keys * HD * heads_here,
        bytes_accessed=2 * width * (4 * rows + 4 * keys),
        transcendentals=rows * keys * heads_here,
    )


ON_CHIP = pl.BlockSpec(memory_space=pltpu.VMEM)
GRANT = 20 * 2**20
SCALARS = pl.BlockSpec(memory_space=pltpu.SMEM)


def side(kernel, lens, operands, outs, scores):
    width = outs[0][1]
    return pl.pallas_call(
        kernel,
        in_specs=[SCALARS] + [ON_CHIP] * len(operands),
        out_specs=[ON_CHIP] * len(outs),
        out_shape=[jax.ShapeDtypeStruct(shape, jnp.bfloat16) for shape in outs],
        scratch_shapes=[pltpu.VMEM(scores, jnp.float32)],
        compiler_params=pltpu.CompilerParams(vmem_limit_bytes=GRANT),
        cost_estimate=cost(*scores, width),
        interpret=INTERPRET,
    )(lens, *operands)


def gather_kernel(runs, spreads, group, dq, th, t1, t2, out):
    rows, slim = dq.shape[0], out.shape[2]
    for run in range(runs):
        here = slice(run * 2 * group, (run + 1) * 2 * group)
        values = [dq[here]]
        for start in (0, rows):
            there = slice(start + here.start, start + here.stop)
            total = th[there].astype(jnp.float32) + t1[there].astype(jnp.float32)
            values.append((total + t2[there].astype(jnp.float32)).astype(jnp.bfloat16))
        for spread in range(spreads):
            cols = slice(spread * slim, (spread + 1) * slim)
            for late in range(2):
                for j, value in enumerate(values):
                    left = (late * 3 + j) * group
                    out[run * spreads + spread, left : left + group] = value[
                        late * group : (late + 1) * group, cols
                    ]


def gather(dq, th, t1, t2, runs, spreads, group):
    return pl.pallas_call(
        functools.partial(gather_kernel, runs, spreads, group),
        in_specs=[ON_CHIP] * 4,
        out_specs=ON_CHIP,
        out_shape=jax.ShapeDtypeStruct(
            (runs * spreads, 6 * group, dq.shape[1] // spreads), jnp.bfloat16
        ),
        compiler_params=pltpu.CompilerParams(vmem_limit_bytes=GRANT // 4),
        cost_estimate=pl.CostEstimate(flops=0, bytes_accessed=16 * dq.size, transcendentals=0),
        name="gather",
        interpret=INTERPRET,
    )(dq, th, t1, t2)


def place_kernel(spread, index, x, out):
    for frame in range(x.shape[0]):
        if spread:
            out[index[frame]] = x[frame]
        else:
            out[frame] = x[index[frame]]


def place(index, x, spread):
    return pl.pallas_call(
        functools.partial(place_kernel, spread),
        in_specs=[SCALARS, ON_CHIP],
        out_specs=ON_CHIP,
        out_shape=jax.ShapeDtypeStruct(x.shape, x.dtype),
        compiler_params=pltpu.CompilerParams(vmem_limit_bytes=GRANT // 4),
        cost_estimate=pl.CostEstimate(flops=0, bytes_accessed=4 * x.size, transcendentals=0),
        name="place",
        interpret=INTERPRET,
    )(index, x)


def assemble_kernel(runs, spreads, group, x, *outs):
    slim = x.shape[2]
    for run in range(runs):
        for spread in range(spreads):
            for core in range(2):
                piece = (run * spreads + spread) * 2 + core
                for j, out in enumerate(outs):
                    left = (core * spreads + spread) * slim
                    out[0, run * group : (run + 1) * group, left : left + slim] = x[
                        piece, j * group : (j + 1) * group, :
                    ]


def assemble(x, runs, spreads, group):
    shape = (1, runs * group, 2 * spreads * x.shape[2])
    return pl.pallas_call(
        functools.partial(assemble_kernel, runs, spreads, group),
        in_specs=[ON_CHIP],
        out_specs=[ON_CHIP] * 3,
        out_shape=[jax.ShapeDtypeStruct(shape, jnp.bfloat16)] * 3,
        compiler_params=pltpu.CompilerParams(vmem_limit_bytes=GRANT),
        name="assemble",
        interpret=INTERPRET,
    )(x)


def shards(vid_q, vid_k, vid_v, vid_dout, aud_q, aud_k, aud_v, aud_dout, aud_len, match):
    frames = lax.axis_size("frame")
    count = lax.axis_size("seq")
    block_here = lax.axis_index("seq")
    core = block_here % 2
    video_rows, width = vid_q.shape[1], vid_q.shape[2]
    audio_rows = aud_q.shape[1]
    half = width // 2
    group = 4 * video_rows // frames
    runs = frames // 4
    spreads = frames // runs
    slim = half // spreads

    pairs = [
        [f * count + 2 * c + k for f in range(frames) for k in range(2)]
        for c in range(count // 2)
    ]

    def pair_exchange(x):
        return lax.all_to_all(
            x, ("frame", "seq"), split_axis=0, concat_axis=0, tiled=True, axis_index_groups=pairs
        )

    def exchange(x):
        return lax.all_to_all(x, "frame", split_axis=0, concat_axis=0, tiled=True)

    def shift(x, by):
        return lax.ppermute(
            x, "seq", [(i, i + by) for i in range(count) if 0 <= i + by < count]
        )

    def swap(x):
        return lax.ppermute(x, "seq", [(i, i ^ 1) for i in range(count)])

    packed = jnp.concatenate([vid_q[0], vid_k[0], vid_v[0], vid_dout[0]], axis=0)
    packed = packed.reshape(frames, group, 2, half).transpose(0, 2, 1, 3)
    spread = pair_exchange(packed.reshape(2 * frames, group, half))
    spread = place(match, spread.reshape(frames, 2 * group, half), True)
    video = exchange(spread).reshape(frames * 2 * group, half)

    def halves(x):
        low, high = x[0, :, :half], x[0, :, half:]
        return jnp.where(core == 0, low, high), jnp.where(core == 0, high, low)

    own_k, send_k = halves(aud_k)
    own_v, send_v = halves(aud_v)
    send_q = halves(aud_q)[1]
    send_g = halves(aud_dout)[1]
    sent = jnp.concatenate([send_q, send_k, send_v, send_g], axis=0)
    theirs = swap(sent)
    audio_here = jnp.concatenate(
        [
            own_k,
            theirs[audio_rows : 2 * audio_rows],
            own_v,
            theirs[2 * audio_rows : 3 * audio_rows],
        ],
        axis=0,
    )
    audio_before = shift(audio_here, 2)
    audio_after = shift(audio_here, -2)

    block = 2 * video_rows
    video_here = video[block : 3 * block]
    video_before = shift(video_here, 2)
    video_after = shift(video_here, -2)
    grad_vq, shared = side(
        functools.partial(video_kernel, group, count),
        aud_len,
        (video, audio_before, audio_here, audio_after),
        [(block, half), (2 * block + 3 * STAT_ROWS, half)],
        (block, 6 * audio_rows),
    )
    grad_aq, video_tb, video_th, video_ta = side(
        functools.partial(audio_whole, group, count),
        aud_len,
        (aud_q[0], aud_dout[0], theirs, video_before, video_here, video_after),
        [(2 * audio_rows, half)] + [(2 * block, half)] * 3,
        (2 * audio_rows, 3 * block),
    )

    from_after, from_before = shift(video_tb, -2), shift(video_ta, 2)
    grads = gather(grad_vq, video_th, from_after, from_before, runs, spreads, group)
    grads = exchange(grads)
    grads = place(match, grads, False)
    grads = pair_exchange(grads.reshape(2 * frames, 3 * group, slim))
    grads = assemble(grads, runs, spreads, group)

    shared_before, shared_after = shift(shared, 2), shift(shared, -2)
    (grad_akv,) = side(
        functools.partial(terms_kernel, group, count),
        aud_len,
        (shared_before, shared, shared_after, audio_here),
        [(4 * audio_rows, half)],
        (3 * block, 2 * audio_rows),
    )
    mine = (
        grad_aq[:audio_rows],
        grad_akv[:audio_rows],
        grad_akv[2 * audio_rows : 3 * audio_rows],
    )
    back = jnp.concatenate(
        [
            grad_aq[audio_rows:],
            grad_akv[audio_rows : 2 * audio_rows],
            grad_akv[3 * audio_rows :],
        ],
        axis=0,
    )
    back = swap(back)

    def whole(own, other):
        return jnp.where(
            core == 0,
            jnp.concatenate([own, other], axis=1),
            jnp.concatenate([other, own], axis=1),
        )[None]

    outs = [
        whole(mine[j], back[j * audio_rows : (j + 1) * audio_rows]) for j in range(3)
    ]
    return (*grads, *outs)


def solution(mesh):
    tokens = P("frame", "seq", None)
    return jax.shard_map(
        shards,
        mesh=mesh,
        in_specs=(tokens,) * 8 + (P(), P()),
        out_specs=(tokens,) * 6,
        check_vma=False,
    )
```

```python
import functools

import jax
import jax.numpy as jnp
from jax import lax
from jax.experimental import pallas as pl
from jax.experimental.pallas import tpu as pltpu
from jax.sharding import PartitionSpec as P


HD = 128
BAND = 2
NEG_BIG = -1e30
FACTOR = HD ** (-0.5)
INTERPRET = False


def contract(left, right, left_dim, right_dim):
    return lax.dot_general(
        left,
        right,
        (((left_dim,), (right_dim,)), ((), ())),
        preferred_element_type=jnp.float32,
    )


def attend_turned(queries, keys, values, grads, bias):
    total = len(queries)
    scores, grad_weights, half, grad_scores, results = {}, {}, {}, {}, []
    for step in range(total + 2):
        if step < total:
            scores[step] = contract(keys[step], queries[step], 1, 1) * FACTOR + bias[...]
            grad_weights[step] = contract(values[step], grads[step], 1, 1)
        h = step - 1
        if 0 <= h < total:
            exponent = jnp.exp(scores[h] - jnp.max(scores[h], axis=0, keepdims=True))
            weights = exponent * (1.0 / jnp.sum(exponent, axis=0, keepdims=True))
            half[h] = weights.astype(jnp.bfloat16)
            delta = jnp.sum(
                half[h].astype(jnp.float32) * grad_weights[h], axis=0, keepdims=True
            )
            grad_scores[h] = (weights * (grad_weights[h] - delta)).astype(jnp.bfloat16)
        h = step - 2
        if 0 <= h < total:
            key_terms = contract(grad_scores[h], queries[h], 1, 0) * FACTOR
            value_terms = contract(half[h], grads[h], 1, 0)
            results.append((contract(grad_scores[h], keys[h], 0, 0) * FACTOR, key_terms, value_terms))
    return zip(*results)


def attend(queries, keys, values, grads, bias):
    total = range(len(queries))
    scores = [contract(queries[h], keys[h], 1, 1) * FACTOR + bias[...] for h in total]
    largest = [jnp.max(scores[h], axis=-1, keepdims=True) for h in total]
    exponent = [jnp.exp(scores[h] - largest[h]) for h in total]
    inverse = [1.0 / jnp.sum(exponent[h], axis=-1, keepdims=True) for h in total]
    weights = [exponent[h] * inverse[h] for h in total]
    half = [weights[h].astype(jnp.bfloat16) for h in total]
    grad_weights = [contract(grads[h], values[h], 1, 1) for h in total]
    delta = [
        jnp.sum(half[h].astype(jnp.float32) * grad_weights[h], axis=-1, keepdims=True)
        for h in total
    ]
    grad_scores = [
        (weights[h] * (grad_weights[h] - delta[h])).astype(jnp.bfloat16) for h in total
    ]
    grad_query = [contract(grad_scores[h], keys[h], 1, 0) * FACTOR for h in total]
    return grad_query, half, grad_scores, (largest, inverse, delta)


def terms(queries, grads, half, grad_scores):
    total = range(len(queries))
    value_terms = [contract(half[h], grads[h], 0, 0) for h in total]
    key_terms = [contract(grad_scores[h], queries[h], 0, 0) * FACTOR for h in total]
    return key_terms, value_terms


def split_stats(value):
    high = value.astype(jnp.bfloat16)
    rest = value - high.astype(jnp.float32)
    middle = rest.astype(jnp.bfloat16)
    low = (rest - middle.astype(jnp.float32)).astype(jnp.bfloat16)
    return high, middle, low


def windows(refs, part, cols):
    keys = jnp.concatenate([ref[:part, cols] for ref in refs], axis=0)
    values = jnp.concatenate([ref[part:, cols] for ref in refs], axis=0)
    return keys, values


def head_spans(wide):
    return [slice(h * HD, (h + 1) * HD) for h in range(wide // HD)]


STAT_ROWS = 8


def video_kernel(group, count, lens, video, before, here, after, dq_ref, out, bias):
    rows = video.shape[0] // 4
    part = before.shape[0] // 2
    video_bias(group, count, lens, part, bias)
    spans = head_spans(dq_ref.shape[1])
    keys, values = zip(*[windows((before, here, after), part, cols) for cols in spans])
    queries = [video[:rows, cols] for cols in spans]
    grads = [video[3 * rows :, cols] for cols in spans]
    grad_query, _, _, stats = attend(queries, keys, values, grads, bias)
    lane = lax.broadcasted_iota(jnp.int32, (rows, HD), 1)
    table = jnp.zeros((rows, HD), jnp.float32)
    for j, stat in enumerate(stats):
        for h, value in enumerate(stat):
            table = jnp.where(lane == j * len(spans) + h, value, table)
    for cols, dq in zip(spans, grad_query, strict=True):
        dq_ref[:, cols] = dq.astype(jnp.bfloat16)
    out[:rows] = video[:rows]
    out[rows : 2 * rows] = video[3 * rows :]
    for j, piece in enumerate(split_stats(table)):
        top = 2 * rows + j * STAT_ROWS
        for k in range(rows // STAT_ROWS):
            out[top : top + STAT_ROWS, k * HD : (k + 1) * HD] = piece[
                k * STAT_ROWS : (k + 1) * STAT_ROWS
            ]


def terms_kernel(group, count, lens, before, here, after, audio, dkv_ref, bias):
    rows = (before.shape[0] - 3 * STAT_ROWS) // 2
    part = audio.shape[0] // 2
    slots = part // 2
    frame = lax.axis_index("frame")
    block = lax.axis_index("seq")
    core = lax.rem(block, 2)
    base = block - core
    place = lax.broadcasted_iota(jnp.int32, (3 * rows, 1), 0)
    offset = 2 * (place // rows) - 2 + (place // group) % 2
    known = (base + offset >= 0) & (base + offset < count)
    column = lax.broadcasted_iota(jnp.int32, (1, part), 1)
    mine = column < slots
    slot = jnp.where(mine, column, column - slots)
    live = slot < jnp.where(mine, lens[frame, block], lens[frame, base + 1 - core])
    own = jnp.where(mine, core, 1 - core)
    near = jnp.where(known, 0.0, NEG_BIG) + jnp.where(live, 0.0, NEG_BIG)
    bias[...] = jnp.where(jnp.abs(offset - own) <= BAND, near, NEG_BIG)
    refs = (before, here, after)
    spans = head_spans(dkv_ref.shape[1])
    total = range(len(spans))
    queries = [jnp.concatenate([ref[:rows, cols] for ref in refs], axis=0) for cols in spans]
    grads = [
        jnp.concatenate([ref[rows : 2 * rows, cols] for ref in refs], axis=0) for cols in spans
    ]
    tables = []
    for ref in refs:
        value = 0.0
        for j in range(3):
            top = 2 * rows + j * STAT_ROWS
            wide = ref[top : top + STAT_ROWS, : rows // STAT_ROWS * HD].astype(jnp.float32)
            value = value + wide
        for k in range(rows // STAT_ROWS):
            tables.append(value[:, k * HD : (k + 1) * HD])
    table = jnp.concatenate(tables, axis=0)
    largest, inverse, delta = [
        [table[:, j * len(spans) + h : j * len(spans) + h + 1] for h in total] for j in range(3)
    ]
    scores = [contract(queries[h], audio[:part, spans[h]], 1, 1) * FACTOR + bias[...] for h in total]
    weights = [jnp.exp(scores[h] - largest[h]) * inverse[h] for h in total]
    half = [weights[h].astype(jnp.bfloat16) for h in total]
    grad_weights = [contract(grads[h], audio[part:, spans[h]], 1, 1) for h in total]
    grad_scores = [
        (weights[h] * (grad_weights[h] - delta[h])).astype(jnp.bfloat16) for h in total
    ]
    key_terms, value_terms = terms(queries, grads, half, grad_scores)
    for h in total:
        dkv_ref[:part, spans[h]] = key_terms[h].astype(jnp.bfloat16)
        dkv_ref[part:, spans[h]] = value_terms[h].astype(jnp.bfloat16)


def video_bias(group, count, lens, part, bias):
    rows, slots = bias.shape[0], part // 2
    frame = lax.axis_index("frame")
    block = lax.axis_index("seq")
    core = lax.rem(block, 2)
    base = block - core
    column = lax.broadcasted_iota(jnp.int32, (1, 3 * part), 1)
    early_row = jnp.full((1, 3 * part), NEG_BIG, jnp.float32)
    late_row = early_row
    for place in range(6):
        offset = 2 * (place // 2) - 2 + (core if place % 2 == 0 else 1 - core)
        time = base + offset
        known = (time >= 0) & (time < count)
        live = lens[frame, jnp.clip(time, 0, count - 1)]
        live = jnp.where(known, live, 0)
        early = jnp.where(jnp.abs(offset) <= BAND, live, 0)
        late = jnp.where(jnp.abs(offset - 1) <= BAND, live, 0)
        first = column >= place * slots
        early_row = jnp.where(first & (column < place * slots + early), 0.0, early_row)
        late_row = jnp.where(first & (column < place * slots + late), 0.0, late_row)
    is_late = (lax.broadcasted_iota(jnp.int32, (rows, 1), 0) // group) % 2
    bias[...] = jnp.where(is_late == 0, early_row, late_row)


def audio_whole(group, count, lens, aud_q, aud_g, theirs, *refs):
    rows = aud_q.shape[0]
    audio_kernel(
        group, count, lens, aud_q, aud_g, theirs.at[:rows], theirs.at[3 * rows :], *refs
    )


def audio_kernel(
    group, count, lens, aud_q, aud_g, their_q, their_g, before, here, after, dq_ref, tb, th, ta, bias
):
    rows, half = aud_q.shape[0], aud_q.shape[1] // 2
    wide = their_q.shape[1]
    part = before.shape[0] // 2
    frame = lax.axis_index("frame")
    block = lax.axis_index("seq")
    core = lax.rem(block, 2)
    base = block - core
    other = base + 1 - core
    key = lax.broadcasted_iota(jnp.int32, (3 * part, 1), 0)
    offset = 2 * (key // part) - 2 + (key // group) % 2
    known = (base + offset >= 0) & (base + offset < count)
    query = lax.broadcasted_iota(jnp.int32, (1, 2 * rows), 1)
    own = jnp.where(query < rows, core, 1 - core)
    near = jnp.where(known, 0.0, NEG_BIG)
    bias[...] = jnp.where(jnp.abs(offset - own) <= BAND, near, NEG_BIG)
    slot = lax.broadcasted_iota(jnp.int32, (rows, 1), 0)
    live_mine = (slot < lens[frame, block]).astype(jnp.float32)
    live_other = (slot < lens[frame, other]).astype(jnp.float32)

    spans = head_spans(wide)
    queries, grads = [], []
    for head, cols in enumerate(spans):
        start = core * half + head * HD
        mine = pl.ds(pl.multiple_of(start, HD), HD)
        queries.append(jnp.concatenate([aud_q[:, mine], their_q[:, cols]], axis=0))
        kept = [
            jnp.where(live > 0, rows_of.astype(jnp.float32), 0.0)
            for live, rows_of in ((live_mine, aud_g[:, mine]), (live_other, their_g[:, cols]))
        ]
        grads.append(jnp.concatenate(kept, axis=0).astype(jnp.bfloat16))
    keys, values = zip(*[windows((before, here, after), part, cols) for cols in spans])
    grad_query, key_terms, value_terms = attend_turned(queries, keys, values, grads, bias)
    for h, cols in enumerate(spans):
        dq_ref[:, cols] = grad_query[h].astype(jnp.bfloat16)
        for place, out in enumerate((tb, th, ta)):
            span = slice(place * part, (place + 1) * part)
            out[:part, cols] = key_terms[h][span].astype(jnp.bfloat16)
            out[part:, cols] = value_terms[h][span].astype(jnp.bfloat16)


def cost(rows, keys, width):
    heads_here = width // HD
    return pl.CostEstimate(
        flops=10 * rows * keys * HD * heads_here,
        bytes_accessed=2 * width * (4 * rows + 4 * keys),
        transcendentals=rows * keys * heads_here,
    )


ON_CHIP = pl.BlockSpec(memory_space=pltpu.VMEM)
GRANT = 20 * 2**20
SCALARS = pl.BlockSpec(memory_space=pltpu.SMEM)


def side(kernel, lens, operands, outs, scores):
    width = outs[0][1]
    return pl.pallas_call(
        kernel,
        in_specs=[SCALARS] + [ON_CHIP] * len(operands),
        out_specs=[ON_CHIP] * len(outs),
        out_shape=[jax.ShapeDtypeStruct(shape, jnp.bfloat16) for shape in outs],
        scratch_shapes=[pltpu.VMEM(scores, jnp.float32)],
        compiler_params=pltpu.CompilerParams(vmem_limit_bytes=GRANT),
        cost_estimate=cost(*scores, width),
        interpret=INTERPRET,
    )(lens, *operands)


def gather_kernel(runs, spreads, group, dq, th, t1, t2, out):
    rows, slim = dq.shape[0], out.shape[2]
    for run in range(runs):
        here = slice(run * 2 * group, (run + 1) * 2 * group)
        values = [dq[here]]
        for start in (0, rows):
            there = slice(start + here.start, start + here.stop)
            total = th[there].astype(jnp.float32) + t1[there].astype(jnp.float32)
            values.append((total + t2[there].astype(jnp.float32)).astype(jnp.bfloat16))
        for spread in range(spreads):
            cols = slice(spread * slim, (spread + 1) * slim)
            for late in range(2):
                for j, value in enumerate(values):
                    left = (late * 3 + j) * group
                    out[run * spreads + spread, left : left + group] = value[
                        late * group : (late + 1) * group, cols
                    ]


def gather(dq, th, t1, t2, runs, spreads, group):
    return pl.pallas_call(
        functools.partial(gather_kernel, runs, spreads, group),
        in_specs=[ON_CHIP] * 4,
        out_specs=ON_CHIP,
        out_shape=jax.ShapeDtypeStruct(
            (runs * spreads, 6 * group, dq.shape[1] // spreads), jnp.bfloat16
        ),
        compiler_params=pltpu.CompilerParams(vmem_limit_bytes=GRANT // 4),
        cost_estimate=pl.CostEstimate(flops=0, bytes_accessed=16 * dq.size, transcendentals=0),
        name="gather",
        interpret=INTERPRET,
    )(dq, th, t1, t2)


def place_kernel(spread, index, x, out, sems):
    copies = []
    for frame in range(x.shape[0]):
        source = x.at[frame] if spread else x.at[index[frame]]
        target = out.at[index[frame]] if spread else out.at[frame]
        copies.append(pltpu.make_async_copy(source, target, sems.at[frame]))
    for copy in copies:
        copy.start()
    for copy in copies:
        copy.wait()


def place(index, x, spread):
    return pl.pallas_call(
        functools.partial(place_kernel, spread),
        in_specs=[SCALARS, ON_CHIP],
        out_specs=pl.BlockSpec(memory_space=pl.ANY),
        scratch_shapes=[pltpu.SemaphoreType.DMA((x.shape[0],))],
        out_shape=jax.ShapeDtypeStruct(x.shape, x.dtype),
        compiler_params=pltpu.CompilerParams(vmem_limit_bytes=GRANT // 4),
        cost_estimate=pl.CostEstimate(flops=0, bytes_accessed=4 * x.size, transcendentals=0),
        name="place",
        interpret=INTERPRET,
    )(index, x)


def assemble_kernel(runs, spreads, group, x, *outs):
    slim = x.shape[2]
    for run in range(runs):
        for spread in range(spreads):
            for core in range(2):
                piece = (run * spreads + spread) * 2 + core
                for j, out in enumerate(outs):
                    left = (core * spreads + spread) * slim
                    out[0, run * group : (run + 1) * group, left : left + slim] = x[
                        piece, j * group : (j + 1) * group, :
                    ]


def assemble(x, runs, spreads, group):
    shape = (1, runs * group, 2 * spreads * x.shape[2])
    return pl.pallas_call(
        functools.partial(assemble_kernel, runs, spreads, group),
        in_specs=[ON_CHIP],
        out_specs=[ON_CHIP] * 3,
        out_shape=[jax.ShapeDtypeStruct(shape, jnp.bfloat16)] * 3,
        compiler_params=pltpu.CompilerParams(vmem_limit_bytes=GRANT),
        name="assemble",
        interpret=INTERPRET,
    )(x)


def shards(vid_q, vid_k, vid_v, vid_dout, aud_q, aud_k, aud_v, aud_dout, aud_len, match):
    frames = lax.axis_size("frame")
    count = lax.axis_size("seq")
    block_here = lax.axis_index("seq")
    core = block_here % 2
    video_rows, width = vid_q.shape[1], vid_q.shape[2]
    audio_rows = aud_q.shape[1]
    half = width // 2
    group = 4 * video_rows // frames
    runs = frames // 4
    spreads = frames // runs
    slim = half // spreads

    pairs = [
        [f * count + 2 * c + k for f in range(frames) for k in range(2)]
        for c in range(count // 2)
    ]

    def pair_exchange(x):
        return lax.all_to_all(
            x, ("frame", "seq"), split_axis=0, concat_axis=0, tiled=True, axis_index_groups=pairs
        )

    def exchange(x):
        return lax.all_to_all(x, "frame", split_axis=0, concat_axis=0, tiled=True)

    def shift(x, by):
        return lax.ppermute(
            x, "seq", [(i, i + by) for i in range(count) if 0 <= i + by < count]
        )

    def swap(x):
        return lax.ppermute(x, "seq", [(i, i ^ 1) for i in range(count)])

    packed = jnp.concatenate([vid_q[0], vid_k[0], vid_v[0], vid_dout[0]], axis=0)
    packed = packed.reshape(frames, group, 2, half).transpose(0, 2, 1, 3)
    spread = pair_exchange(packed.reshape(2 * frames, group, half))
    spread = place(match, spread.reshape(frames, 2 * group, half), True)
    video = exchange(spread).reshape(frames * 2 * group, half)

    def halves(x):
        low, high = x[0, :, :half], x[0, :, half:]
        return jnp.where(core == 0, low, high), jnp.where(core == 0, high, low)

    own_k, send_k = halves(aud_k)
    own_v, send_v = halves(aud_v)
    send_q = halves(aud_q)[1]
    send_g = halves(aud_dout)[1]
    sent = jnp.concatenate([send_q, send_k, send_v, send_g], axis=0)
    theirs = swap(sent)
    audio_here = jnp.concatenate(
        [
            own_k,
            theirs[audio_rows : 2 * audio_rows],
            own_v,
            theirs[2 * audio_rows : 3 * audio_rows],
        ],
        axis=0,
    )
    audio_before = shift(audio_here, 2)
    audio_after = shift(audio_here, -2)

    block = 2 * video_rows
    video_here = video[block : 3 * block]
    video_before = shift(video_here, 2)
    video_after = shift(video_here, -2)
    grad_vq, shared = side(
        functools.partial(video_kernel, group, count),
        aud_len,
        (video, audio_before, audio_here, audio_after),
        [(block, half), (2 * block + 3 * STAT_ROWS, half)],
        (block, 6 * audio_rows),
    )
    grad_aq, video_tb, video_th, video_ta = side(
        functools.partial(audio_whole, group, count),
        aud_len,
        (aud_q[0], aud_dout[0], theirs, video_before, video_here, video_after),
        [(2 * audio_rows, half)] + [(2 * block, half)] * 3,
        (3 * block, 2 * audio_rows),
    )

    from_after, from_before = shift(video_tb, -2), shift(video_ta, 2)
    grads = gather(grad_vq, video_th, from_after, from_before, runs, spreads, group)
    grads = exchange(grads)
    grads = place(match, grads, False)
    grads = pair_exchange(grads.reshape(2 * frames, 3 * group, slim))
    grads = assemble(grads, runs, spreads, group)

    shared_before, shared_after = shift(shared, 2), shift(shared, -2)
    (grad_akv,) = side(
        functools.partial(terms_kernel, group, count),
        aud_len,
        (shared_before, shared, shared_after, audio_here),
        [(4 * audio_rows, half)],
        (3 * block, 2 * audio_rows),
    )
    mine = (
        grad_aq[:audio_rows],
        grad_akv[:audio_rows],
        grad_akv[2 * audio_rows : 3 * audio_rows],
    )
    back = jnp.concatenate(
        [
            grad_aq[audio_rows:],
            grad_akv[audio_rows : 2 * audio_rows],
            grad_akv[3 * audio_rows :],
        ],
        axis=0,
    )
    back = swap(back)

    def whole(own, other):
        return jnp.where(
            core == 0,
            jnp.concatenate([own, other], axis=1),
            jnp.concatenate([other, own], axis=1),
        )[None]

    outs = [
        whole(mine[j], back[j * audio_rows : (j + 1) * audio_rows]) for j in range(3)
    ]
    return (*grads, *outs)


def solution(mesh):
    tokens = P("frame", "seq", None)
    return jax.shard_map(
        shards,
        mesh=mesh,
        in_specs=(tokens,) * 8 + (P(), P()),
        out_specs=(tokens,) * 6,
        check_vma=False,
    )
```
